256 devices in a mesh: cfg: 2 (over y_hi), req: 16 (over z, core), tp: 8 (over y_lo, x).
Axes of the slice: x: 4, y: 4 (y_hi: 2, y_lo: 2; y = y_hi * 2 + y_lo), z: 8, core: 2. Of those that a mesh axis runs over, the one named last changes fastest.
Arguments:
- img_hidden: bfloat16 [2, 8192, 3072], P('cfg', 'req'), may hold values from -0.3125 to 0.3125
- txt_hidden: bfloat16 [2, 2048, 3072], P('cfg', 'req'), may hold values from -6 to 6
- latent: float32 [8192, 64], P(('req', 'tp', 'cfg')), may hold values from -6 to 6
- segment: int32 [8192], P('req'), may hold values from 0 to 3, never falling along the last dimension, each value on 1 to 4096 neighbouring positions
- timestep: int32 [4], replicated, may hold values from 0 to 27
- mod_weight: bfloat16 [256, 5, 3072], P('req'), may hold values from -0.375 to 0.375
- qkv_weight: bfloat16 [3072, 3, 3072], P('req', None, 'tp'), may hold values from -0.109375 to 0.109375
- txt_kv_weight: bfloat16 [3072, 2, 3072], P('req', None, 'tp'), may hold values from -0.109375 to 0.109375
- out_weight: bfloat16 [3072, 3072], P('tp'), may hold values from -0.109375 to 0.109375
- final_weight: bfloat16 [3072, 64], replicated, may hold values from -0.109375 to 0.109375
Outputs:
- guided: float32 [8192, 64], P(('req', 'tp', 'cfg'))
- latent_next: float32 [8192, 64], P(('req', 'tp', 'cfg'))
The draws below stay inside these ranges and needn't reach their ends.
Inputs may be any that keep to these rules, and one draw needn't show every extreme that they name: `segment`: image rows of one request are consecutive and request numbers never fall along the rows; every one of the 4 requests has 1 to 4096 rows, one exactly 4096.
All inputs are finite; a program needn't handle non-finite values.
Results may differ from the reference program's by a relative error of at most 0.04.
Values may be sent and summed in bfloat16 or wider, within the bound.
A program may use at most 128 MiB of HBM per device.

```python
import math
import jax
import jax.numpy as jnp
import numpy as np
from jax import lax

D = 3072
HEADS = 24
HD = 128
TEMB = 256
PATCH = 64
TXT = 512
STEPS = 28
IMG_DEV = 512
REQS = 4
IMG = 8192
MAXLEN = 4096
N_REQ = 16


def plant(array, own_key, low, top_value):
    spot = [jax.random.randint(jax.random.fold_in(own_key, axis), (), 0, length) for axis, length in enumerate(array.shape)]
    widest = array.shape.index(max(array.shape))
    neighbour = spot[:widest] + [(spot[widest] + 1) % array.shape[widest]] + spot[widest + 1:]
    return array.at[tuple(spot)].set(low).at[tuple(neighbour)].set(top_value)


def shard_levels(rng, dims, split, low, high):
    level = 1.0
    for dim, blocks in split:
        steps = jax.random.uniform(jax.random.fold_in(jax.random.fold_in(rng, 6), dim), (blocks,), jnp.float32, low / len(split), high / len(split))
        level = level * jnp.repeat(jnp.exp(steps), dims[dim] // blocks).reshape((-1,) + (1,) * (len(dims) - 1 - dim))
    return level


def split_up(number_of, total, bound, slope):
    loads = [(1 << 20) // math.isqrt(grade ** slope) + 1 for grade in range(2, number_of + 1)]
    surplus, given = total - bound - (number_of - 1), [1] * (number_of - 1)
    while surplus > 0:
        candidates = [i for i in range(number_of - 1) if given[i] < bound]
        mass, left = sum([loads[i] for i in candidates]), surplus
        for i in candidates:
            more = min(bound - given[i], max(1, left * loads[i] // mass), surplus)
            given[i] = given[i] + more
            surplus = surplus - more
    return np.array([bound] + given)


def uneven_parts(own_key, amount, total, bound, lean):
    if amount == 2:
        one = jax.random.randint(own_key, (), max(1, total - bound), min(bound, total - 1) + 1)
        return jnp.stack([one, total - one])
    sizes = jnp.asarray(split_up(amount, total, bound, lean), jnp.int32)
    pairs = (amount - 1) // 2
    source_of, receiver = sizes[1:1 + 2 * pairs:2], sizes[2:2 + 2 * pairs:2]
    slack = jnp.minimum(source_of - 1, bound - receiver)
    passed = jax.random.randint(jax.random.fold_in(own_key, 1), (pairs,), 0, 1 << 20) % (slack + 1)
    sizes = sizes.at[1:1 + 2 * pairs:2].set(source_of - passed).at[2:2 + 2 * pairs:2].set(receiver + passed)
    return sizes[jax.random.permutation(jax.random.fold_in(own_key, 2), amount)]


def bell_draw(rng, extent, spread, most, shards=(), held_as=jnp.bfloat16):
    result = jax.random.normal(rng, extent, jnp.float32) * spread
    if len(shards) > 0:
        result = shard_levels(rng, extent, shards, -0.22, 0.18) * result
    return jnp.clip(result, min=-most, max=most).astype(held_as)


def setup_inputs(seed: int = 0) -> dict:
    seeds = jax.random.split(jax.random.key(seed), 11)
    return {
        "img_hidden": bell_draw(seeds[0], (2, IMG, D), 0.05, 0.3125, ((0, 2), (1, 16))),
        "txt_hidden": bell_draw(seeds[1], (2, REQS * TXT, D), 1.0, 6.0, ((0, 2), (1, 16))),
        "latent": bell_draw(seeds[2], (IMG, PATCH), 1.0, 6.0, ((0, 256),), jnp.float32),
        "segment": jnp.searchsorted(jnp.cumsum(uneven_parts(seeds[3], REQS, IMG, MAXLEN, 2)), jnp.arange(IMG), side="right").astype(jnp.int32),
        "timestep": plant(jax.random.randint(seeds[4], (REQS,), 0, STEPS), jax.random.fold_in(seeds[4], 1), 0, STEPS - 1).astype(jnp.int32),
        "mod_weight": bell_draw(seeds[5], (TEMB, 5, D), TEMB ** -0.5, 0.375, ((0, 16),)),
        "qkv_weight": bell_draw(seeds[6], (D, 3, HEADS * HD), D ** -0.5, 0.109375, ((0, 16), (2, 8))),
        "txt_kv_weight": bell_draw(seeds[7], (D, 2, HEADS * HD), D ** -0.5, 0.109375, ((0, 16), (2, 8))),
        "out_weight": bell_draw(seeds[8], (HEADS * HD, D), (HEADS * HD) ** -0.5, 0.109375, ((0, 8),)),
        "final_weight": bell_draw(seeds[9], (D, PATCH), D ** -0.5, 0.109375),
    }


GUIDE_SCALE = 4.0

def sigma_table():
    linear_grid = 1.0 - jnp.arange(STEPS + 1, dtype=jnp.float32) / STEPS
    return 3.0 * linear_grid / (1.0 + 2.0 * linear_grid)

def time_features(sigmas):
    half_width = TEMB // 2
    frequency = jnp.exp(-jnp.log(10000.0) * jnp.arange(half_width, dtype=jnp.float32) / half_width)
    angles = 1000.0 * sigmas[:, None] * frequency[None, :]
    features = jnp.concatenate([jnp.cos(angles), jnp.sin(angles)], axis=1)
    return jax.nn.silu(features).astype(jnp.bfloat16)

def layer_norm(hidden):
    hidden = hidden.astype(jnp.float32)
    center = hidden - lax.optimization_barrier(jnp.mean(hidden, axis=-1, keepdims=True))
    return center * lax.rsqrt(lax.optimization_barrier(jnp.mean(center * center, axis=-1, keepdims=True)) + 1e-06)

def rms_norm(hidden):
    return (hidden * lax.rsqrt(lax.optimization_barrier(jnp.mean(hidden * hidden, axis=-1, keepdims=True)) + 1e-06)).astype(jnp.bfloat16)

def select_rows(labels, count, table):
    onehot = (labels[:, None] == jnp.arange(count, dtype=jnp.int32)[None, :]).astype(jnp.float32)
    return jnp.dot(onehot, table, precision=lax.Precision.HIGHEST)

def modulate(hidden, labels, shift, scale):
    normed = layer_norm(hidden)
    return (normed * (1.0 + select_rows(labels, REQS, scale)) + select_rows(labels, REQS, shift)).astype(jnp.bfloat16)

def attention(queries, keys, values, segment, labels):
    scale = HD ** (-0.5)
    query_blocks = queries.reshape(N_REQ, IMG_DEV, HEADS, HD)
    label_blocks = segment.reshape(N_REQ, IMG_DEV)
    keys_wide = keys.astype(jnp.float32)
    values_wide = values.astype(jnp.float32)

    def one_block(inputs):
        block, block_labels = inputs
        scores = jnp.einsum('qhd,khd->hqk', block.astype(jnp.float32), keys_wide) * scale
        allowed = block_labels[:, None] == labels[None, :]
        weights = jnp.where(allowed[None], jnp.exp(scores), 0.0)
        denom = lax.optimization_barrier(jnp.sum(weights, axis=2)).T
        numer = jnp.einsum('hqk,khd->qhd', weights.astype(jnp.bfloat16).astype(jnp.float32), values_wide)
        return (numer / denom[:, :, None]).astype(jnp.bfloat16)
    return lax.map(one_block, (query_blocks, label_blocks)).reshape(IMG, HEADS * HD)

def half_velocity(image, text, segment, modulation, qkv_weight, txt_kv_weight, out_weight, final_weight):
    width = HEADS * HD
    text_labels = jnp.arange(REQS * TXT, dtype=jnp.int32) // TXT
    image_in = modulate(image, segment, modulation[:, 0], modulation[:, 1])
    text_in = modulate(text, text_labels, modulation[:, 3], modulation[:, 4])
    image_proj = jnp.dot(image_in, qkv_weight.reshape(D, 3 * width), preferred_element_type=jnp.float32)
    text_proj = jnp.dot(text_in, txt_kv_weight.reshape(D, 2 * width), preferred_element_type=jnp.float32)
    queries = rms_norm(image_proj[:, :width].reshape(IMG, HEADS, HD))
    keys = jnp.concatenate([rms_norm(image_proj[:, width:2 * width].reshape(IMG, HEADS, HD)), rms_norm(text_proj[:, :width].reshape(REQS * TXT, HEADS, HD))], axis=0)
    values = jnp.concatenate([image_proj[:, 2 * width:].astype(jnp.bfloat16).reshape(IMG, HEADS, HD), text_proj[:, width:].astype(jnp.bfloat16).reshape(REQS * TXT, HEADS, HD)], axis=0)
    labels = jnp.concatenate([segment, text_labels], axis=0)
    attended = attention(queries, keys, values, segment, labels)
    update = jnp.dot(attended, out_weight, preferred_element_type=jnp.float32)
    stream = image.astype(jnp.float32) + select_rows(segment, REQS, modulation[:, 2]) * update
    return jnp.dot(layer_norm(stream).astype(jnp.bfloat16), final_weight, preferred_element_type=jnp.float32)

def reference(img_hidden, txt_hidden, latent, segment, timestep, mod_weight, qkv_weight, txt_kv_weight, out_weight, final_weight):
    table = sigma_table()
    sig_now = jnp.take(table, timestep)
    sig_next = jnp.take(table, timestep + 1)
    features = time_features(sig_now)
    modulation = jnp.dot(features, mod_weight.reshape(TEMB, 5 * D), preferred_element_type=jnp.float32).reshape(REQS, 5, D)
    cond_velocity = half_velocity(img_hidden[0], txt_hidden[0], segment, modulation, qkv_weight, txt_kv_weight, out_weight, final_weight)
    uncond_velocity = half_velocity(img_hidden[1], txt_hidden[1], segment, modulation, qkv_weight, txt_kv_weight, out_weight, final_weight)
    guided = uncond_velocity + GUIDE_SCALE * (cond_velocity - uncond_velocity)
    step_size = select_rows(segment, REQS, (sig_next - sig_now)[:, None])[:, 0]
    return (guided, latent + step_size[:, None] * guided)
```

```python
import functools
import math

import jax
import jax.numpy as jnp
from jax import lax
from jax.experimental import pallas as pl
from jax.experimental.pallas import tpu as pltpu
from jax.sharding import PartitionSpec as P

HD = 128
TEMB = 256
TXT = 512
STEPS = 28
REQS = 4
GUIDE_SCALE = 4.0
MESH = pl.DeviceIdType.MESH
VMEM_LIMIT = 66_000_000


def sigma_table():
    linear_grid = 1.0 - jnp.arange(STEPS + 1, dtype=jnp.float32) / STEPS
    return 3.0 * linear_grid / (1.0 + 2.0 * linear_grid)


def time_features(sigmas):
    half_width = TEMB // 2
    frequency = jnp.exp(-jnp.log(10000.0) * jnp.arange(half_width, dtype=jnp.float32) / half_width)
    angles = 1000.0 * sigmas[:, None] * frequency[None, :]
    features = jnp.concatenate([jnp.cos(angles), jnp.sin(angles)], axis=1)
    return jax.nn.silu(features).astype(jnp.bfloat16)


def rms_heads(value):
    parts = []
    for h in range(value.shape[1] // HD):
        part = value[:, h * HD : (h + 1) * HD]
        mean = jnp.mean(part * part, axis=-1, keepdims=True)
        parts.append((part * lax.rsqrt(mean + 1e-06)).astype(jnp.bfloat16))
    return jnp.concatenate(parts, axis=1)


class Ring:
    def __init__(self, own, held, z, c, chips, sems):
        self.own, self.held, self.z, self.c, self.chips = own, held, z, c, chips
        self.send, self.recv, self.sib_send, self.sib_recv = sems
        self.half = held.shape[1] // 2

    def rows(self, h):
        return pl.ds(h * self.half, self.half)

    def copy(self, d, s, h):
        sign = 1 if d == 0 else -1
        origin = lax.rem(self.z - sign * (s - 1) + self.chips, self.chips)
        target = lax.rem(self.z + sign + self.chips, self.chips)
        slot = self.held.at[2 * origin + self.c, self.rows(h)]
        source = self.own.at[self.rows(h)] if s == 1 else slot
        return pltpu.make_async_remote_copy(
            source,
            slot,
            self.send.at[d, s - 1, h],
            self.recv.at[d, s - 1, h],
            device_id={"req": 2 * target + self.c},
            device_id_type=MESH,
        )

    def arrived(self, d, s, h):
        sign = 1 if d == 0 else -1
        origin = lax.rem(self.z - sign * s + self.chips, self.chips)
        slot = self.held.at[2 * origin + self.c, self.rows(h)]
        return pltpu.make_async_remote_copy(
            slot,
            slot,
            self.send.at[d, s - 1, h],
            self.recv.at[d, s - 1, h],
            device_id={"req": 2 * self.z + 1 - self.c},
            device_id_type=MESH,
        )

    def origin(self, k):
        step = (k + 1) // 2
        sign = 1 if k % 2 == 1 else -1
        return lax.rem(self.z - sign * step + self.chips, self.chips)

    def sibling(self, k, h, core):
        slot = self.held.at[2 * self.origin(k) + core, self.rows(h)]
        source = self.own.at[self.rows(h)] if k == 0 else slot
        return pltpu.make_async_remote_copy(
            source,
            slot,
            self.sib_send.at[k, h],
            self.sib_recv.at[k, h],
            device_id={"req": 2 * self.z + 1 - self.c},
            device_id_type=MESH,
        )

    def start(self):
        for h in range(2):
            for d in range(2):
                self.copy(d, 1, h).start()
        for h in range(2):
            self.sibling(0, h, self.c).start()

    def poll(self, s, h):
        last = self.chips // 2
        for d in range(2):
            if s == last and h != d:
                continue
            self.arrived(d, s, h).wait_recv()
            if s + 1 < last or (s + 1 == last and h == d):
                self.copy(d, s + 1, h).start()
            self.sibling(2 * s - 1 + (d if s < last else 0), h, self.c).start()

    def take(self, k):
        for h in range(2):
            self.sibling(k, h, 1 - self.c).wait_recv()

    def finish(self):
        last = self.chips // 2
        for s in range(1, last + 1):
            for h in range(2):
                for d in range(2):
                    if s < last or h == d:
                        self.copy(d, s, h).wait_send()
        for k in range(self.chips):
            for h in range(2):
                self.sibling(k, h, self.c).wait_send()


def ring_sems(chips):
    return [
        pltpu.SemaphoreType.DMA((2, chips // 2, 2)),
        pltpu.SemaphoreType.DMA((2, chips // 2, 2)),
        pltpu.SemaphoreType.DMA((chips, 2)),
        pltpu.SemaphoreType.DMA((chips, 2)),
    ]


def project_kernel(
    peers,
    w_ref,
    image_ref,
    text_ref,
    label_row_ref,
    label_ref,
    partial_ref,
    q_ref,
    kv_ref,
    labels_ref,
    mod_ref,
    held,
    image,
    text,
    ready,
    text_ready,
    acc,
    text_acc,
    parts,
    mod,
    labels,
    send,
    recv,
    sib_send,
    sib_recv,
    part_send,
    part_recv,
    mod_send,
    mod_recv,
    lab_send,
    lab_recv,
    local,
):
    me = lax.axis_index("req")
    z, c = me // 2, lax.rem(me, 2)
    chips = peers // 2
    rows, width = image.shape
    text_rows = text.shape[0]
    head_width = q_ref.shape[1]
    wide = width // chips

    barrier = pltpu.get_barrier_semaphore()
    for k in range(1, peers):
        pl.semaphore_signal(
            barrier, inc=1, device_id={"req": lax.rem(me + k, peers)}, device_id_type=MESH
        )
    pl.semaphore_wait(barrier, peers - 1)

    ring = Ring(w_ref, held, z, c, chips, (send, recv, sib_send, sib_recv))

    def part_copy(k):
        target = lax.rem(me + k, peers)
        return pltpu.make_async_remote_copy(
            partial_ref.at[target], parts.at[k], part_send.at[k], part_recv.at[k],
            device_id={"req": target}, device_id_type=MESH,
        )

    def mod_copy(k, owner):
        return pltpu.make_async_remote_copy(
            mod.at[owner], mod.at[owner], mod_send.at[k], mod_recv.at[k],
            device_id={"req": lax.rem(me + k, peers)}, device_id_type=MESH,
        )

    def label_copy(k, owner):
        return pltpu.make_async_remote_copy(
            label_row_ref, labels.at[owner], lab_send.at[k], lab_recv.at[k],
            device_id={"req": lax.rem(me + k, peers)}, device_id_type=MESH,
        )

    for k in range(1, peers):
        part_copy(k).start()
    ring.start()
    own_part = pltpu.make_async_copy(partial_ref.at[me], parts.at[0], local.at[0])
    own_part.start()
    image_in = pltpu.make_async_copy(image_ref, image, local.at[1])
    image_in.start()
    text_in = pltpu.make_async_copy(text_ref, text, local.at[2])
    text_in.start()
    own_w = pltpu.make_async_copy(w_ref, held.at[me], local.at[3])
    own_w.start()
    own_label = pltpu.make_async_copy(label_row_ref, labels.at[me], local.at[4])
    own_label.start()
    for k in range(1, peers):
        label_copy(k, me).start()

    own_part.wait()
    for k in range(1, peers):
        part_copy(k).wait_recv()
    total = parts[0]
    for k in range(1, peers):
        total = total + parts[k]
    mod[me] = total
    for k in range(1, peers):
        mod_copy(k, me).start()
    image_in.wait()
    text_in.wait()
    for k in range(1, peers):
        mod_copy(k, lax.rem(me - k + peers, peers)).wait_recv()

    def mod_row(request, component, chunk):
        return mod[2 * chunk + request // 2, 5 * (request % 2) + component : 5 * (request % 2) + component + 1, :]

    tile = 32

    def image_tile(i, carry):
        span = pl.ds(i * tile, tile)
        value = image[span, :].astype(jnp.float32)
        center = value - jnp.mean(value, axis=-1, keepdims=True)
        rstd = lax.rsqrt(jnp.mean(center * center, axis=-1, keepdims=True) + 1e-06)
        label = label_ref[span, :]
        for chunk in range(chips):
            shift = mod_row(REQS - 1, 0, chunk)
            scale = mod_row(REQS - 1, 1, chunk)
            for request in range(REQS - 2, -1, -1):
                mine = label == request
                shift = jnp.where(mine, mod_row(request, 0, chunk), shift)
                scale = jnp.where(mine, mod_row(request, 1, chunk), scale)
            part = center[:, chunk * wide : (chunk + 1) * wide] * rstd
            ready[chunk, span, :] = (part * (1.0 + scale) + shift).astype(jnp.bfloat16)
        return carry

    text_request = me * text_rows // TXT
    text_base = text_request // 2
    text_half = 5 * lax.rem(text_request, 2)

    def text_tile(i, carry):
        span = pl.ds(i * tile, tile)
        value = text[span, :].astype(jnp.float32)
        center = value - jnp.mean(value, axis=-1, keepdims=True)
        rstd = lax.rsqrt(jnp.mean(center * center, axis=-1, keepdims=True) + 1e-06)
        for chunk in range(chips):
            shift = mod[2 * chunk + text_base, pl.ds(text_half + 3, 1), :]
            scale = mod[2 * chunk + text_base, pl.ds(text_half + 4, 1), :]
            part = center[:, chunk * wide : (chunk + 1) * wide] * rstd
            text_ready[chunk, span, :] = (part * (1.0 + scale) + shift).astype(jnp.bfloat16)
        return carry

    image_width = 3 * head_width
    block = w_ref.shape[0]
    mtile = 128

    def multiply(k):
        chip = ring.origin(k)

        def one(i, carry):
            span = pl.ds(i * mtile, mtile)
            lhs = ready[chip, span, :]
            rhs = held[pl.ds(2 * chip, 2), :, :image_width].reshape(2 * block, image_width)
            product = jnp.dot(lhs, rhs, preferred_element_type=jnp.float32)
            acc[span, :] = product if k == 0 else acc[span, :] + product
            return carry

        lax.fori_loop(0, rows // mtile, one, 0)
        text_product = jnp.dot(
            text_ready[chip],
            held[pl.ds(2 * chip, 2), :, image_width:].reshape(2 * block, 2 * head_width),
            preferred_element_type=jnp.float32,
        )
        text_acc[...] = text_product if k == 0 else text_acc[...] + text_product

    lax.fori_loop(0, text_rows // tile, text_tile, 0)
    ring.poll(1, 0)
    lax.fori_loop(0, rows // tile // 2, image_tile, 0)
    ring.poll(1, 1)
    lax.fori_loop(rows // tile // 2, rows // tile, image_tile, 0)
    own_w.wait()
    ring.take(0)
    multiply(0)
    last = chips // 2
    for s in range(2, last + 1):
        ring.poll(s, 0)
        ring.take(2 * s - 3)
        multiply(2 * s - 3)
        ring.poll(s, 1)
        ring.take(2 * s - 2)
        multiply(2 * s - 2)
    ring.take(chips - 1)
    multiply(chips - 1)

    def finish_tile(i, carry):
        span = pl.ds(i * mtile, mtile)
        q_ref[span, :] = rms_heads(acc[span, :head_width])
        kv_ref[span, :head_width] = rms_heads(acc[span, head_width : 2 * head_width])
        kv_ref[span, head_width:] = acc[span, 2 * head_width :].astype(jnp.bfloat16)
        return carry

    lax.fori_loop(0, rows // mtile, finish_tile, 0)
    kv_ref[rows:, :head_width] = rms_heads(text_acc[:, :head_width])
    kv_ref[rows:, head_width:] = text_acc[:, head_width:].astype(jnp.bfloat16)
    own_label.wait()
    for k in range(1, peers):
        label_copy(k, lax.rem(me - k + peers, peers)).wait_recv()
    labels_ref[...] = labels[...]
    mod_ref[...] = mod[...]
    for k in range(1, peers):
        part_copy(k).wait_send()
        mod_copy(k, me).wait_send()
        label_copy(k, me).wait_send()
    ring.finish()


def attend_kernel(
    peers,
    kv_ref,
    out_w_ref,
    image_ref,
    q_ref,
    label_ref,
    labels_ref,
    mod_ref,
    final_ref,
    latent_ref,
    dsig_ref,
    guided_ref,
    next_ref,
    held,
    out_w,
    numer,
    denom,
    attended,
    gathered,
    update,
    image,
    velocity,
    other_velocity,
    send,
    recv,
    sib_send,
    sib_recv,
    x_send,
    x_recv,
    y_send,
    y_recv,
    ws_send,
    ws_recv,
    a_send,
    a_recv,
    v_send,
    v_recv,
    local,
):
    me = lax.axis_index("req")
    tp = lax.axis_index("tp")
    cfg = lax.axis_index("cfg")
    z, c = me // 2, lax.rem(me, 2)
    chips = peers // 2
    y, x = tp // 4, lax.rem(tp, 4)
    rows, head_width = q_ref.shape
    heads = head_width // HD
    block = held.shape[1]
    right = lax.rem(x + 1, 4)
    left = lax.rem(x + 3, 4)
    flip = lax.rem(tp + 4, 8)

    barrier = pltpu.get_barrier_semaphore()
    greet = [
        {"req": 2 * lax.rem(z + 1, chips) + c},
        {"req": 2 * lax.rem(z + chips - 1, chips) + c},
        {"req": 2 * z + 1 - c},
        {"cfg": 1 - cfg, "tp": flip},
        {"cfg": 1 - cfg},
    ] + [{"tp": lax.rem(tp + k, 8)} for k in range(1, 8)]
    for peer in greet:
        pl.semaphore_signal(barrier, inc=1, device_id=peer, device_id_type=MESH)
    pl.semaphore_wait(barrier, len(greet))

    ring = Ring(kv_ref, held, z, c, chips, (send, recv, sib_send, sib_recv))
    ring.start()
    own_kv = pltpu.make_async_copy(kv_ref, held.at[me], local.at[0])
    own_kv.start()

    piece = out_w.shape[1] // 4

    def w_rows(core, h):
        return pl.ds(core * 2 * piece + h * piece, piece)

    def w_copy(source, shard, core, h, sems, index, peer):
        slot = out_w.at[shard, w_rows(core, h)]
        return pltpu.make_async_remote_copy(
            slot if source is None else source,
            slot,
            sems[0].at[index],
            sems[1].at[index],
            device_id=peer,
            device_id_type=MESH,
        )

    xs, ys, ws = (x_send, x_recv), (y_send, y_recv), (ws_send, ws_recv)
    across = [x, left, right, lax.rem(x + 2, 4)]
    to_right, to_left = {"tp": y * 4 + right}, {"tp": y * 4 + left}
    to_y = [{"tp": flip}, {"cfg": 1 - cfg, "tp": flip}]
    to_sibling = {"req": 2 * z + 1 - c}
    own_piece = [out_w_ref.at[w_rows(c, h)] for h in range(2)]

    def x_copy(d, h):
        return w_copy(own_piece[h], tp, c, h, xs, 2 * d + h, to_right if d == 0 else to_left)

    def x_arrived(d, h):
        return w_copy(None, y * 4 + (left if d == 0 else right), c, h, xs, 2 * d + h, to_sibling)

    def x_forward(d):
        return w_copy(None, y * 4 + (left if d == 0 else right), c, d, xs, 4 + d, to_right if d == 0 else to_left)

    def x_forwarded(d):
        return w_copy(None, y * 4 + across[3], c, d, xs, 4 + d, to_sibling)

    def y_copy(n, h):
        return w_copy(own_piece[h] if n == 0 else None, y * 4 + across[n], c, h, ys, 2 * n + h, to_y[h])

    def y_arrived(n, h):
        return w_copy(None, (1 - y) * 4 + across[n], c, h, ys, 2 * n + h, to_sibling)

    def w_sibling(n, h, core):
        shard = y * 4 + across[n] if n < 4 else (1 - y) * 4 + across[n - 4]
        return w_copy(None, shard, core, h, ws, 2 * n + h, to_sibling)

    for h in range(2):
        for d in range(2):
            x_copy(d, h).start()
        y_copy(0, h).start()
    own_out = pltpu.make_async_copy(out_w_ref, out_w.at[tp], local.at[1])
    own_out.start()
    out_rows = rows // 8
    own_image = pltpu.make_async_copy(
        image_ref.at[pl.ds(tp * out_rows, out_rows)], image, local.at[2]
    )
    own_image.start()
    numer[...] = jnp.zeros_like(numer)
    denom[...] = jnp.zeros_like(denom)

    def x_events():
        for h in range(2):
            for d in range(2):
                x_arrived(d, h).wait_recv()
                if h == d:
                    x_forward(d).start()
                y_copy(1 + d, h).start()
                w_sibling(1 + d, h, c).start()

    def x_more():
        for d in range(2):
            x_forwarded(d).wait_recv()
            y_copy(3, d).start()
            w_sibling(3, d, c).start()

    def y_events(n):
        for h in range(2):
            y_arrived(n, h).wait_recv()
            w_sibling(4 + n, h, c).start()

    factor = HD ** (-0.5) * math.log2(math.e)
    qtile = 128
    text_keys = block - rows

    def attend(k):
        chip = ring.origin(k)

        def one(i, carry):
            b = 2 * chip + i // (rows // qtile)
            span = pl.ds(lax.rem(i, rows // qtile) * qtile, qtile)
            text_label = jnp.full((1, text_keys), b * text_keys // TXT, jnp.int32)
            key_label = jnp.concatenate([labels_ref[b], text_label], axis=1)
            allowed = label_ref[span, :] == key_label
            for h in range(heads):
                q = q_ref[span, h * HD : (h + 1) * HD]
                key = held[b, :, h * HD : (h + 1) * HD]
                value = held[b, :, head_width + h * HD : head_width + (h + 1) * HD]
                scores = lax.dot_general(
                    q, key, (((1,), (1,)), ((), ())), preferred_element_type=jnp.float32
                )
                weights = jnp.where(allowed, jnp.exp2(scores * factor), 0.0)
                part = weights[:, :HD]
                for j in range(1, block // HD):
                    part = part + weights[:, j * HD : (j + 1) * HD]
                denom[h, span, :] += part
                numer[h, span, :] += jnp.dot(
                    weights.astype(jnp.bfloat16), value, preferred_element_type=jnp.float32
                )
            return carry

        lax.fori_loop(0, 2 * (rows // qtile), one, 0)

    own_kv.wait()
    ring.take(0)
    attend(0)
    ring.poll(1, 0)
    ring.poll(1, 1)
    last = chips // 2
    for s in range(2, last + 1):
        ring.poll(s, 0)
        if s == 2:
            x_events()
        ring.take(2 * s - 3)
        attend(2 * s - 3)
        if s == 3:
            x_more()
            y_events(0)
        ring.poll(s, 1)
        ring.take(2 * s - 2)
        attend(2 * s - 2)
        if s == 3:
            y_events(1)
            y_events(2)
    y_events(3)
    ring.take(chips - 1)
    attend(chips - 1)

    for h in range(heads):
        total = jnp.sum(denom[h], axis=-1, keepdims=True)
        value = (numer[h] / total).astype(jnp.bfloat16)
        for t in range(8):
            attended[t, :, h * HD : (h + 1) * HD] = value[t * out_rows : (t + 1) * out_rows]

    def a_copy(k, owner):
        target = lax.rem(tp + k, 8)
        return pltpu.make_async_remote_copy(
            attended.at[target], gathered.at[owner], a_send.at[k], a_recv.at[k],
            device_id={"tp": target}, device_id_type=MESH,
        )

    for k in range(1, 8):
        a_copy(k, tp).start()
    gathered[tp] = attended[tp]

    own_out.wait()
    own_image.wait()
    for n in range(1, 8):
        for h in range(2):
            w_sibling(n, h, 1 - c).wait_recv()
    update[...] = jnp.dot(gathered[tp], out_w[tp], preferred_element_type=jnp.float32)
    for k in range(1, 8):
        a_copy(k, lax.rem(tp - k + 8, 8)).wait_recv()

    def add_shard(k, carry):
        t = lax.rem(tp + k, 8)
        update[...] += jnp.dot(gathered[t], out_w[t], preferred_element_type=jnp.float32)
        return carry

    lax.fori_loop(1, 8, add_shard, 0)

    width = update.shape[1]
    wide = width // chips
    label = label_ref[pl.ds(pl.multiple_of(tp * out_rows, out_rows), out_rows), :]
    masks = [label == request for request in range(REQS - 1)]
    mean = jnp.zeros((out_rows, 1), jnp.float32)
    for chunk in range(chips):
        cols = slice(chunk * wide, (chunk + 1) * wide)

        def gate_row(request):
            row = 5 * (request % 2) + 2
            return mod_ref[2 * chunk + request // 2, row : row + 1, :]

        gate = gate_row(REQS - 1)
        for request in range(REQS - 2, -1, -1):
            gate = jnp.where(masks[request], gate_row(request), gate)
        stream = image[:, cols].astype(jnp.float32) + gate * update[:, cols]
        update[:, cols] = stream
        mean = mean + jnp.sum(stream, axis=-1, keepdims=True)
    center = update[...] - mean / width
    normed = center * lax.rsqrt(jnp.mean(center * center, axis=-1, keepdims=True) + 1e-06)
    velocity[...] = jnp.dot(
        normed.astype(jnp.bfloat16), final_ref[...], preferred_element_type=jnp.float32
    )
    half_rows = out_rows // 2
    sent = pl.ds(pl.multiple_of((1 - cfg) * half_rows, half_rows), half_rows)
    kept = pl.ds(pl.multiple_of(cfg * half_rows, half_rows), half_rows)
    swap = pltpu.make_async_remote_copy(
        velocity.at[sent], other_velocity, v_send, v_recv,
        device_id={"cfg": 1 - cfg}, device_id_type=MESH,
    )
    swap.start()
    own = velocity[kept, :]
    own_label = label_ref[pl.ds(pl.multiple_of(tp * out_rows + cfg * half_rows, half_rows), half_rows), :]
    step = jnp.where(
        own_label == 0,
        dsig_ref[0],
        jnp.where(own_label == 1, dsig_ref[1], jnp.where(own_label == 2, dsig_ref[2], dsig_ref[3])),
    )
    swap.wait()
    other = other_velocity[...]
    first = cfg == 0
    cond = jnp.where(first, own, other)
    uncond = jnp.where(first, other, own)
    guided = uncond + GUIDE_SCALE * (cond - uncond)
    guided_ref[...] = guided
    next_ref[...] = latent_ref[...] + step * guided

    for h in range(2):
        for d in range(2):
            x_copy(d, h).wait_send()
    for d in range(2):
        x_forward(d).wait_send()
    for n in range(4):
        for h in range(2):
            y_copy(n, h).wait_send()
    for n in range(1, 8):
        for h in range(2):
            w_sibling(n, h, c).wait_send()
    for k in range(1, 8):
        a_copy(k, tp).wait_send()
    ring.finish()


def per_device(
    peers,
    img_hidden,
    txt_hidden,
    latent,
    segment,
    timestep,
    mod_weight,
    qkv_weight,
    txt_kv_weight,
    out_weight,
    final_weight,
):
    image = img_hidden[0]
    text = txt_hidden[0]
    rows, width = image.shape
    text_rows = text.shape[0]
    shard, comps = mod_weight.shape[:2]
    chips = peers // 2
    wide = width // chips
    head_width = qkv_weight.shape[2]
    block_rows = rows + text_rows
    table = sigma_table()
    sig_now = jnp.take(table, timestep)
    sig_next = jnp.take(table, timestep + 1)
    features = time_features(sig_now)
    feature_part = lax.dynamic_slice_in_dim(features, lax.axis_index("req") * shard, shard, 1)
    partial_mod = jnp.einsum(
        "rj,jkd->rkd", feature_part, mod_weight, preferred_element_type=jnp.float32
    )
    partial_mod = (
        partial_mod.reshape(2, 2 * comps, chips, wide).transpose(2, 0, 1, 3)
    ).reshape(peers, 2 * comps, wide)
    weights = jnp.concatenate(
        [
            qkv_weight.reshape(qkv_weight.shape[0], 3 * head_width),
            txt_kv_weight.reshape(qkv_weight.shape[0], 2 * head_width),
        ],
        axis=1,
    )
    label_row = segment.reshape(1, rows)
    label = segment.reshape(rows, 1)
    any_spec = pl.BlockSpec(memory_space=pl.ANY)
    vmem = pl.BlockSpec(memory_space=pltpu.VMEM)
    dma = pltpu.SemaphoreType.DMA
    queries, key_values, labels, mod = pl.pallas_call(
        functools.partial(project_kernel, peers),
        out_shape=(
            jax.ShapeDtypeStruct((rows, head_width), jnp.bfloat16),
            jax.ShapeDtypeStruct((block_rows, 2 * head_width), jnp.bfloat16),
            jax.ShapeDtypeStruct((peers, 1, rows), jnp.int32),
            jax.ShapeDtypeStruct((peers, 2 * comps, wide), jnp.float32),
        ),
        in_specs=[any_spec, any_spec, any_spec, vmem, vmem, vmem],
        out_specs=(vmem, vmem, vmem, vmem),
        scratch_shapes=[
            pltpu.VMEM((peers, weights.shape[0], weights.shape[1]), jnp.bfloat16),
            pltpu.VMEM((rows, width), jnp.bfloat16),
            pltpu.VMEM((text_rows, width), jnp.bfloat16),
            pltpu.VMEM((chips, rows, wide), jnp.bfloat16),
            pltpu.VMEM((chips, text_rows, wide), jnp.bfloat16),
            pltpu.VMEM((rows, 3 * head_width), jnp.float32),
            pltpu.VMEM((text_rows, 2 * head_width), jnp.float32),
            pltpu.VMEM((peers, 2 * comps, wide), jnp.float32),
            pltpu.VMEM((peers, 2 * comps, wide), jnp.float32),
            pltpu.VMEM((peers, 1, rows), jnp.int32),
            *ring_sems(chips),
            *[dma((peers,)) for _ in range(6)],
            dma((5,)),
        ],
        compiler_params=pltpu.CompilerParams(
            collective_id=0, has_side_effects=True, vmem_limit_bytes=VMEM_LIMIT
        ),
        name="project",
    )(weights, image, text, label_row, label, partial_mod)
    out_rows = rows // 8
    half_rows = out_rows // 2
    return tuple(
        pl.pallas_call(
            functools.partial(attend_kernel, peers),
            out_shape=(
                jax.ShapeDtypeStruct(latent.shape, jnp.float32),
                jax.ShapeDtypeStruct(latent.shape, jnp.float32),
            ),
            in_specs=[any_spec, any_spec, any_spec]
            + [vmem] * 6
            + [pl.BlockSpec(memory_space=pltpu.SMEM)],
            out_specs=(vmem, vmem),
            scratch_shapes=[
                pltpu.VMEM((peers, block_rows, 2 * head_width), jnp.bfloat16),
                pltpu.VMEM((8, head_width, width), jnp.bfloat16),
                pltpu.VMEM((head_width // HD, rows, HD), jnp.float32),
                pltpu.VMEM((head_width // HD, rows, HD), jnp.float32),
                pltpu.VMEM((8, out_rows, head_width), jnp.bfloat16),
                pltpu.VMEM((8, out_rows, head_width), jnp.bfloat16),
                pltpu.VMEM((out_rows, width), jnp.float32),
                pltpu.VMEM((out_rows, width), jnp.bfloat16),
                pltpu.VMEM((out_rows, latent.shape[1]), jnp.float32),
                pltpu.VMEM((half_rows, latent.shape[1]), jnp.float32),
                *ring_sems(chips),
                dma((6,)),
                dma((6,)),
                dma((8,)),
                dma((8,)),
                dma((16,)),
                dma((16,)),
                dma((8,)),
                dma((8,)),
                dma,
                dma,
                dma((3,)),
            ],
            compiler_params=pltpu.CompilerParams(
                collective_id=1, has_side_effects=True, vmem_limit_bytes=VMEM_LIMIT
            ),
            name="attend",
        )(
            key_values,
            out_weight,
            image,
            queries,
            label,
            labels,
            mod,
            final_weight,
            latent,
            sig_next - sig_now,
        )
    )


def solution(mesh):
    return jax.shard_map(
        functools.partial(per_device, mesh.shape["req"]),
        mesh=mesh,
        in_specs=(
            P("cfg", "req", None),
            P("cfg", "req", None),
            P(("req", "tp", "cfg"), None),
            P("req"),
            P(),
            P("req", None, None),
            P("req", None, "tp"),
            P("req", None, "tp"),
            P("tp", None),
            P(),
        ),
        out_specs=(P(("req", "tp", "cfg"), None), P(("req", "tp", "cfg"), None)),
        check_vma=False,
    )
```

```python
import functools
import math

import jax
import jax.numpy as jnp
from jax import lax
from jax.experimental import pallas as pl
from jax.experimental.pallas import tpu as pltpu
from jax.sharding import PartitionSpec as P

HD = 128
TEMB = 256
TXT = 512
STEPS = 28
REQS = 4
GUIDE_SCALE = 4.0
MESH = pl.DeviceIdType.MESH
VMEM_LIMIT = 66_000_000
LEAD = 32


def sigma_table():
    linear_grid = 1.0 - jnp.arange(STEPS + 1, dtype=jnp.float32) / STEPS
    return 3.0 * linear_grid / (1.0 + 2.0 * linear_grid)


def time_features(sigmas):
    half_width = TEMB // 2
    frequency = jnp.exp(-jnp.log(10000.0) * jnp.arange(half_width, dtype=jnp.float32) / half_width)
    angles = 1000.0 * sigmas[:, None] * frequency[None, :]
    features = jnp.concatenate([jnp.cos(angles), jnp.sin(angles)], axis=1)
    return jax.nn.silu(features).astype(jnp.bfloat16)


def rms_heads(value):
    parts = []
    for h in range(value.shape[1] // HD):
        part = value[:, h * HD : (h + 1) * HD]
        mean = jnp.mean(part * part, axis=-1, keepdims=True)
        parts.append((part * lax.rsqrt(mean + 1e-06)).astype(jnp.bfloat16))
    return jnp.concatenate(parts, axis=1)


class Ring:
    def __init__(self, own, held, z, c, chips, sems, lead=0, cfg=0, pair_sems=None, first=None):
        self.own, self.held, self.z, self.c, self.chips = own, held, z, c, chips
        self.send, self.recv, self.sib_send, self.sib_recv = sems
        self.half = held.shape[1] // 2
        self.first = self.half if first is None else first
        self.lead, self.cfg, self.pair_sems = lead, cfg, pair_sems

    def whole(self, h):
        return pl.ds(0, self.first) if h == 0 else pl.ds(self.first, 2 * self.half - self.first)

    def rows(self, h):
        if not self.lead:
            return self.whole(h)
        start = pl.multiple_of(h * self.half + self.lead * self.cfg, self.lead)
        return pl.ds(start, self.half - self.lead)

    def pair_rows(self, h, cfg):
        start = pl.multiple_of(h * self.half + (self.half - self.lead) * cfg, self.lead)
        return pl.ds(start, self.lead)

    def pair(self, k, h, cfg):
        slot = self.held.at[2 * self.origin(k) + self.c, self.pair_rows(h, cfg)]
        return pltpu.make_async_remote_copy(
            slot,
            slot,
            self.pair_sems[0].at[k, h],
            self.pair_sems[1].at[k, h],
            device_id={"cfg": 1 - self.cfg},
            device_id_type=MESH,
        )

    def pair_sibling(self, k, h, core):
        slot = self.held.at[2 * self.origin(k) + core, self.pair_rows(h, 1 - self.cfg)]
        return pltpu.make_async_remote_copy(
            slot,
            slot,
            self.pair_sems[2].at[k, h],
            self.pair_sems[3].at[k, h],
            device_id={"req": 2 * self.z + 1 - self.c},
            device_id_type=MESH,
        )

    def chunks(self, s, h):
        return [2 * s - 1, 2 * s] if s < self.chips // 2 else [2 * s - 1]

    def relay(self, s, h):
        for k in self.chunks(s, h):
            self.pair(k, h, 1 - self.cfg).wait_recv()
            self.pair_sibling(k, h, self.c).start()

    def copy(self, d, s, h):
        sign = 1 if d == 0 else -1
        origin = lax.rem(self.z - sign * (s - 1) + self.chips, self.chips)
        target = lax.rem(self.z + sign + self.chips, self.chips)
        slot = self.held.at[2 * origin + self.c, self.rows(h)]
        source = self.own.at[self.rows(h)] if s == 1 else slot
        return pltpu.make_async_remote_copy(
            source,
            slot,
            self.send.at[d, s - 1, h],
            self.recv.at[d, s - 1, h],
            device_id={"req": 2 * target + self.c},
            device_id_type=MESH,
        )

    def arrived(self, d, s, h):
        sign = 1 if d == 0 else -1
        origin = lax.rem(self.z - sign * s + self.chips, self.chips)
        slot = self.held.at[2 * origin + self.c, self.rows(h)]
        return pltpu.make_async_remote_copy(
            slot,
            slot,
            self.send.at[d, s - 1, h],
            self.recv.at[d, s - 1, h],
            device_id={"req": 2 * self.z + 1 - self.c},
            device_id_type=MESH,
        )

    def origin(self, k):
        step = (k + 1) // 2
        sign = 1 if k % 2 == 1 else -1
        return lax.rem(self.z - sign * step + self.chips, self.chips)

    def sibling(self, k, h, core):
        rows = self.whole(h) if k == 0 else self.rows(h)
        slot = self.held.at[2 * self.origin(k) + core, rows]
        source = self.own.at[rows] if k == 0 else slot
        return pltpu.make_async_remote_copy(
            source,
            slot,
            self.sib_send.at[k, h],
            self.sib_recv.at[k, h],
            device_id={"req": 2 * self.z + 1 - self.c},
            device_id_type=MESH,
        )

    def start(self):
        for h in range(2):
            for d in range(2):
                self.copy(d, 1, h).start()
        for h in range(2):
            self.sibling(0, h, self.c).start()

    def poll(self, s, h):
        last = self.chips // 2
        for d in range(2):
            if s == last and h != d:
                continue
            self.arrived(d, s, h).wait_recv()
            if s + 1 < last or (s + 1 == last and h == d):
                self.copy(d, s + 1, h).start()
            k = 2 * s - 1 + (d if s < last else 0)
            if self.lead:
                self.pair(k, h, self.cfg).start()
            self.sibling(k, h, self.c).start()

    def take(self, k):
        for h in range(2):
            self.take_half(k, h)

    def take_half(self, k, h):
        self.sibling(k, h, 1 - self.c).wait_recv()
        if self.lead and k:
            self.pair_sibling(k, h, 1 - self.c).wait_recv()

    def finish(self):
        last = self.chips // 2
        for s in range(1, last + 1):
            for h in range(2):
                for d in range(2):
                    if s < last or h == d:
                        self.copy(d, s, h).wait_send()
        for k in range(self.chips):
            for h in range(2):
                self.sibling(k, h, self.c).wait_send()
                if self.lead and k:
                    self.pair(k, h, self.cfg).wait_send()
                    self.pair_sibling(k, h, self.c).wait_send()


def ring_sems(chips):
    return [
        pltpu.SemaphoreType.DMA((2, chips // 2, 2)),
        pltpu.SemaphoreType.DMA((2, chips // 2, 2)),
        pltpu.SemaphoreType.DMA((chips, 2)),
        pltpu.SemaphoreType.DMA((chips, 2)),
    ]


def project_kernel(
    peers,
    w_ref,
    image_ref,
    text_ref,
    label_row_ref,
    label_ref,
    partial_ref,
    q_ref,
    kv_ref,
    labels_ref,
    mod_ref,
    held,
    image,
    text,
    ready,
    text_ready,
    acc,
    text_acc,
    parts,
    mod,
    labels,
    send,
    recv,
    sib_send,
    sib_recv,
    pair_send,
    pair_recv,
    pair_sib_send,
    pair_sib_recv,
    part_send,
    part_recv,
    mod_send,
    mod_recv,
    lab_send,
    lab_recv,
    local,
):
    me = lax.axis_index("req")
    plane = 2 * lax.axis_index("tp") + lax.axis_index("cfg")
    z, c = me // 2, lax.rem(me, 2)
    chips = peers // 2
    rows, width = image.shape
    text_rows = text.shape[0]
    head_width = q_ref.shape[1]
    wide = width // chips

    def in_plane(k):
        target = lax.rem(plane + k, peers)
        return {"tp": target // 2, "cfg": lax.rem(target, 2)}

    barrier = pltpu.get_barrier_semaphore()
    for k in range(1, peers):
        for peer in ({"req": lax.rem(me + k, peers)}, in_plane(k)):
            pl.semaphore_signal(barrier, inc=1, device_id=peer, device_id_type=MESH)
    pl.semaphore_wait(barrier, 2 * (peers - 1))

    ring = Ring(
        w_ref, held, z, c, chips, (send, recv, sib_send, sib_recv), LEAD, lax.axis_index("cfg"),
        (pair_send, pair_recv, pair_sib_send, pair_sib_recv),
    )

    def part_copy(k):
        target = lax.rem(me + k, peers)
        return pltpu.make_async_remote_copy(
            partial_ref.at[plane], parts.at[k], part_send.at[k], part_recv.at[k],
            device_id={"req": target}, device_id_type=MESH,
        )

    def mod_copy(k, owner):
        return pltpu.make_async_remote_copy(
            mod.at[owner], mod.at[owner], mod_send.at[k], mod_recv.at[k],
            device_id=in_plane(k), device_id_type=MESH,
        )

    def label_copy(k, owner):
        return pltpu.make_async_remote_copy(
            label_row_ref, labels.at[owner], lab_send.at[k], lab_recv.at[k],
            device_id={"req": lax.rem(me + k, peers)}, device_id_type=MESH,
        )

    for k in range(1, peers):
        part_copy(k).start()
    ring.start()
    own_part = pltpu.make_async_copy(partial_ref.at[plane], parts.at[0], local.at[0])
    own_part.start()
    image_in = pltpu.make_async_copy(image_ref, image, local.at[1])
    image_in.start()
    text_in = pltpu.make_async_copy(text_ref, text, local.at[2])
    text_in.start()
    own_w = pltpu.make_async_copy(w_ref, held.at[me], local.at[3])
    own_w.start()
    own_label = pltpu.make_async_copy(label_row_ref, labels.at[me], local.at[4])
    own_label.start()
    for k in range(1, peers):
        label_copy(k, me).start()

    own_part.wait()
    for k in range(1, peers):
        part_copy(k).wait_recv()
    total = parts[0]
    for k in range(1, peers):
        total = total + parts[k]
    mod[plane] = total
    for k in range(1, peers):
        mod_copy(k, plane).start()
    image_in.wait()
    text_in.wait()
    for k in range(1, peers):
        mod_copy(k, lax.rem(plane - k + peers, peers)).wait_recv()

    def mod_row(request, component, chunk):
        return mod[2 * chunk + request // 2, 5 * (request % 2) + component : 5 * (request % 2) + component + 1, :]

    tile = 32

    def image_tile(i, carry):
        span = pl.ds(i * tile, tile)
        value = image[span, :].astype(jnp.float32)
        center = value - jnp.mean(value, axis=-1, keepdims=True)
        rstd = lax.rsqrt(jnp.mean(center * center, axis=-1, keepdims=True) + 1e-06)
        label = label_ref[span, :]
        for chunk in range(chips):
            shift = mod_row(REQS - 1, 0, chunk)
            scale = mod_row(REQS - 1, 1, chunk)
            for request in range(REQS - 2, -1, -1):
                mine = label == request
                shift = jnp.where(mine, mod_row(request, 0, chunk), shift)
                scale = jnp.where(mine, mod_row(request, 1, chunk), scale)
            part = center[:, chunk * wide : (chunk + 1) * wide] * rstd
            ready[chunk, span, :] = (part * (1.0 + scale) + shift).astype(jnp.bfloat16)
        return carry

    text_request = me * text_rows // TXT
    text_base = text_request // 2
    text_half = 5 * lax.rem(text_request, 2)

    def text_tile(i, carry):
        span = pl.ds(i * tile, tile)
        value = text[span, :].astype(jnp.float32)
        center = value - jnp.mean(value, axis=-1, keepdims=True)
        rstd = lax.rsqrt(jnp.mean(center * center, axis=-1, keepdims=True) + 1e-06)
        for chunk in range(chips):
            shift = mod[2 * chunk + text_base, pl.ds(text_half + 3, 1), :]
            scale = mod[2 * chunk + text_base, pl.ds(text_half + 4, 1), :]
            part = center[:, chunk * wide : (chunk + 1) * wide] * rstd
            text_ready[chunk, span, :] = (part * (1.0 + scale) + shift).astype(jnp.bfloat16)
        return carry

    image_width = 3 * head_width
    block = w_ref.shape[0]
    mtile = 256

    def multiply(k):
        chip = ring.origin(k)

        def one(i, carry):
            span = pl.ds(i * mtile, mtile)
            lhs = ready[chip, span, :]
            rhs = held[pl.ds(2 * chip, 2), :, :image_width].reshape(2 * block, image_width)
            product = jnp.dot(lhs, rhs, preferred_element_type=jnp.float32)
            acc[span, :] = product if k == 0 else acc[span, :] + product
            return carry

        lax.fori_loop(0, rows // mtile, one, 0)
        text_product = jnp.dot(
            text_ready[chip],
            held[pl.ds(2 * chip, 2), :, image_width:].reshape(2 * block, 2 * head_width),
            preferred_element_type=jnp.float32,
        )
        text_acc[...] = text_product if k == 0 else text_acc[...] + text_product

    lax.fori_loop(0, text_rows // tile, text_tile, 0)
    ring.poll(1, 0)
    lax.fori_loop(0, rows // tile // 2, image_tile, 0)
    ring.poll(1, 1)
    lax.fori_loop(rows // tile // 2, rows // tile, image_tile, 0)
    own_w.wait()
    ring.take(0)
    multiply(0)
    last = chips // 2
    for s in range(2, last + 1):
        ring.poll(s, 0)
        if s == 2:
            ring.relay(1, 0)
        ring.relay(s - 1, 1)
        ring.take(2 * s - 3)
        multiply(2 * s - 3)
        ring.poll(s, 1)
        ring.relay(s, 0)
        ring.take(2 * s - 2)
        multiply(2 * s - 2)
    ring.relay(last, 1)
    ring.take(chips - 1)
    multiply(chips - 1)

    def finish_tile(i, carry):
        span = pl.ds(i * mtile, mtile)
        q_ref[span, :] = rms_heads(acc[span, :head_width])
        kv_ref[span, :head_width] = rms_heads(acc[span, head_width : 2 * head_width])
        kv_ref[span, head_width:] = acc[span, 2 * head_width :].astype(jnp.bfloat16)
        return carry

    lax.fori_loop(0, rows // mtile, finish_tile, 0)
    kv_ref[rows:, :head_width] = rms_heads(text_acc[:, :head_width])
    kv_ref[rows:, head_width:] = text_acc[:, head_width:].astype(jnp.bfloat16)
    own_label.wait()
    for k in range(1, peers):
        label_copy(k, lax.rem(me - k + peers, peers)).wait_recv()
    labels_ref[...] = labels[...]
    mod_ref[...] = mod[...]
    for k in range(1, peers):
        part_copy(k).wait_send()
        mod_copy(k, plane).wait_send()
        label_copy(k, me).wait_send()
    ring.finish()


def attend_kernel(
    peers,
    kv_ref,
    out_w_ref,
    image_ref,
    q_ref,
    label_ref,
    labels_ref,
    mod_ref,
    final_ref,
    latent_ref,
    dsig_ref,
    guided_ref,
    next_ref,
    held,
    out_w,
    numer,
    denom,
    attended,
    gathered,
    update,
    image,
    velocity,
    other_velocity,
    send,
    recv,
    sib_send,
    sib_recv,
    x_send,
    x_recv,
    y_send,
    y_recv,
    ws_send,
    ws_recv,
    a_send,
    a_recv,
    v_send,
    v_recv,
    local,
):
    me = lax.axis_index("req")
    tp = lax.axis_index("tp")
    cfg = lax.axis_index("cfg")
    z, c = me // 2, lax.rem(me, 2)
    chips = peers // 2
    y, x = tp // 4, lax.rem(tp, 4)
    rows, head_width = q_ref.shape
    heads = head_width // HD
    block = held.shape[1]
    right = lax.rem(x + 1, 4)
    left = lax.rem(x + 3, 4)
    flip = lax.rem(tp + 4, 8)

    barrier = pltpu.get_barrier_semaphore()
    greet = [
        {"req": 2 * lax.rem(z + 1, chips) + c},
        {"req": 2 * lax.rem(z + chips - 1, chips) + c},
        {"req": 2 * z + 1 - c},
        {"cfg": 1 - cfg, "tp": flip},
        {"cfg": 1 - cfg},
    ] + [{"tp": lax.rem(tp + k, 8)} for k in range(1, 8)]
    for peer in greet:
        pl.semaphore_signal(barrier, inc=1, device_id=peer, device_id_type=MESH)
    pl.semaphore_wait(barrier, len(greet))

    text_keys = block - rows
    first = 3 * HD
    ring = Ring(kv_ref, held, z, c, chips, (send, recv, sib_send, sib_recv), first=first)
    ring.start()
    own_kv = pltpu.make_async_copy(kv_ref, held.at[me], local.at[0])
    own_kv.start()

    piece = out_w.shape[1] // 4

    def w_rows(core, h):
        return pl.ds(core * 2 * piece + h * piece, piece)

    def w_copy(source, shard, core, h, sems, index, peer):
        slot = out_w.at[shard, w_rows(core, h)]
        return pltpu.make_async_remote_copy(
            slot if source is None else source,
            slot,
            sems[0].at[index],
            sems[1].at[index],
            device_id=peer,
            device_id_type=MESH,
        )

    xs, ys, ws = (x_send, x_recv), (y_send, y_recv), (ws_send, ws_recv)
    across = [x, left, right, lax.rem(x + 2, 4)]
    to_right, to_left = {"tp": y * 4 + right}, {"tp": y * 4 + left}
    to_y = [{"tp": flip}, {"cfg": 1 - cfg, "tp": flip}]
    to_sibling = {"req": 2 * z + 1 - c}
    own_piece = [out_w_ref.at[w_rows(c, h)] for h in range(2)]

    def x_copy(d, h):
        return w_copy(own_piece[h], tp, c, h, xs, 2 * d + h, to_right if d == 0 else to_left)

    def x_arrived(d, h):
        return w_copy(None, y * 4 + (left if d == 0 else right), c, h, xs, 2 * d + h, to_sibling)

    def x_forward(d):
        return w_copy(None, y * 4 + (left if d == 0 else right), c, d, xs, 4 + d, to_right if d == 0 else to_left)

    def x_forwarded(d):
        return w_copy(None, y * 4 + across[3], c, d, xs, 4 + d, to_sibling)

    def y_copy(n, h):
        return w_copy(own_piece[h] if n == 0 else None, y * 4 + across[n], c, h, ys, 2 * n + h, to_y[h])

    def y_arrived(n, h):
        return w_copy(None, (1 - y) * 4 + across[n], c, h, ys, 2 * n + h, to_sibling)

    def w_sibling(n, h, core):
        shard = y * 4 + across[n] if n < 4 else (1 - y) * 4 + across[n - 4]
        return w_copy(None, shard, core, h, ws, 2 * n + h, to_sibling)

    for h in range(2):
        for d in range(2):
            x_copy(d, h).start()
        y_copy(0, h).start()
    own_out = pltpu.make_async_copy(out_w_ref, out_w.at[tp], local.at[1])
    own_out.start()
    out_rows = rows // 8
    own_image = pltpu.make_async_copy(
        image_ref.at[pl.ds(tp * out_rows, out_rows)], image, local.at[2]
    )
    own_image.start()
    numer[...] = jnp.zeros_like(numer)
    denom[...] = jnp.zeros_like(denom)

    def x_events():
        for h in range(2):
            for d in range(2):
                x_arrived(d, h).wait_recv()
                if h == d:
                    x_forward(d).start()
                y_copy(1 + d, h).start()
                w_sibling(1 + d, h, c).start()

    def x_more():
        for d in range(2):
            x_forwarded(d).wait_recv()
            y_copy(3, d).start()
            w_sibling(3, d, c).start()

    def y_events(n):
        for h in range(2):
            y_arrived(n, h).wait_recv()
            w_sibling(4 + n, h, c).start()

    factor = HD ** (-0.5) * math.log2(math.e)
    qtile = 256

    def attend(k, part_of):
        chip = ring.origin(k)
        keys = slice(0, first) if part_of == 0 else slice(first, block)

        def one(i, carry):
            b = 2 * chip + i // (rows // qtile)
            span = pl.ds(lax.rem(i, rows // qtile) * qtile, qtile)
            if part_of == 0:
                key_label = labels_ref[b, :, keys]
            else:
                text_label = jnp.full((1, text_keys), b * text_keys // TXT, jnp.int32)
                key_label = jnp.concatenate([labels_ref[b, :, first:], text_label], axis=1)
            allowed = label_ref[span, :] == key_label
            for h in range(heads):
                q = q_ref[span, h * HD : (h + 1) * HD]
                key = held[b, keys, h * HD : (h + 1) * HD]
                value = held[b, keys, head_width + h * HD : head_width + (h + 1) * HD]
                scores = lax.dot_general(
                    q, key, (((1,), (1,)), ((), ())), preferred_element_type=jnp.float32
                )
                weights = jnp.where(allowed, jnp.exp2(scores * factor), 0.0)
                part = weights[:, :HD]
                for j in range(1, (keys.stop - keys.start) // HD):
                    part = part + weights[:, j * HD : (j + 1) * HD]
                denom[h, span, :] += part
                numer[h, span, :] += jnp.dot(
                    weights.astype(jnp.bfloat16), value, preferred_element_type=jnp.float32
                )
            return carry

        lax.fori_loop(0, 2 * (rows // qtile), one, 0)

    def attend_halves(s, part_of):
        for k in ring.chunks(s, part_of):
            ring.take_half(k, part_of)
            attend(k, part_of)

    last = chips // 2
    own_kv.wait()
    ring.take_half(0, 0)
    attend(0, 0)
    ring.poll(1, 0)
    ring.take_half(0, 1)
    attend(0, 1)
    ring.poll(1, 1)
    attend_halves(1, 0)
    for s in range(2, last):
        ring.poll(s, 0)
        if s == 2:
            x_events()
        attend_halves(s - 1, 1)
        if s == 3:
            x_more()
            y_events(0)
        ring.poll(s, 1)
        attend_halves(s, 0)
        if s == 3:
            y_events(1)
    ring.poll(last, 0)
    attend_halves(last - 1, 1)
    y_events(2)
    attend_halves(last, 0)
    ring.poll(last, 1)
    y_events(3)
    attend_halves(last, 1)

    for h in range(heads):
        total = jnp.sum(denom[h], axis=-1, keepdims=True)
        value = (numer[h] / total).astype(jnp.bfloat16)
        for t in range(8):
            attended[t, :, h * HD : (h + 1) * HD] = value[t * out_rows : (t + 1) * out_rows]

    def a_copy(k, owner):
        target = lax.rem(tp + k, 8)
        return pltpu.make_async_remote_copy(
            attended.at[target], gathered.at[owner], a_send.at[k], a_recv.at[k],
            device_id={"tp": target}, device_id_type=MESH,
        )

    for k in range(1, 8):
        a_copy(k, tp).start()
    gathered[tp] = attended[tp]

    own_out.wait()
    own_image.wait()
    for n in range(1, 8):
        for h in range(2):
            w_sibling(n, h, 1 - c).wait_recv()
    update[...] = jnp.dot(gathered[tp], out_w[tp], preferred_element_type=jnp.float32)
    for k in range(1, 8):
        a_copy(k, lax.rem(tp - k + 8, 8)).wait_recv()

    def add_shard(k, carry):
        t = lax.rem(tp + k, 8)
        update[...] += jnp.dot(gathered[t], out_w[t], preferred_element_type=jnp.float32)
        return carry

    lax.fori_loop(1, 8, add_shard, 0)

    width = update.shape[1]
    wide = width // chips
    label = label_ref[pl.ds(pl.multiple_of(tp * out_rows, out_rows), out_rows), :]
    masks = [label == request for request in range(REQS - 1)]
    mean = jnp.zeros((out_rows, 1), jnp.float32)
    for chunk in range(chips):
        cols = slice(chunk * wide, (chunk + 1) * wide)

        def gate_row(request):
            row = 5 * (request % 2) + 2
            return mod_ref[2 * chunk + request // 2, row : row + 1, :]

        gate = gate_row(REQS - 1)
        for request in range(REQS - 2, -1, -1):
            gate = jnp.where(masks[request], gate_row(request), gate)
        stream = image[:, cols].astype(jnp.float32) + gate * update[:, cols]
        update[:, cols] = stream
        mean = mean + jnp.sum(stream, axis=-1, keepdims=True)
    center = update[...] - mean / width
    normed = center * lax.rsqrt(jnp.mean(center * center, axis=-1, keepdims=True) + 1e-06)
    velocity[...] = jnp.dot(
        normed.astype(jnp.bfloat16), final_ref[...], preferred_element_type=jnp.float32
    )
    half_rows = out_rows // 2
    sent = pl.ds(pl.multiple_of((1 - cfg) * half_rows, half_rows), half_rows)
    kept = pl.ds(pl.multiple_of(cfg * half_rows, half_rows), half_rows)
    swap = pltpu.make_async_remote_copy(
        velocity.at[sent], other_velocity, v_send, v_recv,
        device_id={"cfg": 1 - cfg}, device_id_type=MESH,
    )
    swap.start()
    own = velocity[kept, :]
    own_label = label_ref[pl.ds(pl.multiple_of(tp * out_rows + cfg * half_rows, half_rows), half_rows), :]
    step = jnp.where(
        own_label == 0,
        dsig_ref[0],
        jnp.where(own_label == 1, dsig_ref[1], jnp.where(own_label == 2, dsig_ref[2], dsig_ref[3])),
    )
    swap.wait()
    other = other_velocity[...]
    first = cfg == 0
    cond = jnp.where(first, own, other)
    uncond = jnp.where(first, other, own)
    guided = uncond + GUIDE_SCALE * (cond - uncond)
    guided_ref[...] = guided
    next_ref[...] = latent_ref[...] + step * guided

    for h in range(2):
        for d in range(2):
            x_copy(d, h).wait_send()
    for d in range(2):
        x_forward(d).wait_send()
    for n in range(4):
        for h in range(2):
            y_copy(n, h).wait_send()
    for n in range(1, 8):
        for h in range(2):
            w_sibling(n, h, c).wait_send()
    for k in range(1, 8):
        a_copy(k, tp).wait_send()
    ring.finish()


def per_device(
    peers,
    img_hidden,
    txt_hidden,
    latent,
    segment,
    timestep,
    mod_weight,
    qkv_weight,
    txt_kv_weight,
    out_weight,
    final_weight,
):
    image = img_hidden[0]
    text = txt_hidden[0]
    rows, width = image.shape
    text_rows = text.shape[0]
    shard, comps = mod_weight.shape[:2]
    chips = peers // 2
    wide = width // chips
    head_width = qkv_weight.shape[2]
    block_rows = rows + text_rows
    table = sigma_table()
    sig_now = jnp.take(table, timestep)
    sig_next = jnp.take(table, timestep + 1)
    features = time_features(sig_now)
    feature_part = lax.dynamic_slice_in_dim(features, lax.axis_index("req") * shard, shard, 1)
    partial_mod = jnp.einsum(
        "rj,jkd->rkd", feature_part, mod_weight, preferred_element_type=jnp.float32
    )
    partial_mod = (
        partial_mod.reshape(2, 2 * comps, chips, wide).transpose(2, 0, 1, 3)
    ).reshape(peers, 2 * comps, wide)
    weights = jnp.concatenate(
        [
            qkv_weight.reshape(qkv_weight.shape[0], 3 * head_width),
            txt_kv_weight.reshape(qkv_weight.shape[0], 2 * head_width),
        ],
        axis=1,
    )
    label_row = segment.reshape(1, rows)
    label = segment.reshape(rows, 1)
    any_spec = pl.BlockSpec(memory_space=pl.ANY)
    vmem = pl.BlockSpec(memory_space=pltpu.VMEM)
    dma = pltpu.SemaphoreType.DMA
    queries, key_values, labels, mod = pl.pallas_call(
        functools.partial(project_kernel, peers),
        out_shape=(
            jax.ShapeDtypeStruct((rows, head_width), jnp.bfloat16),
            jax.ShapeDtypeStruct((block_rows, 2 * head_width), jnp.bfloat16),
            jax.ShapeDtypeStruct((peers, 1, rows), jnp.int32),
            jax.ShapeDtypeStruct((peers, 2 * comps, wide), jnp.float32),
        ),
        in_specs=[any_spec, any_spec, any_spec, vmem, vmem, vmem],
        out_specs=(vmem, vmem, vmem, vmem),
        scratch_shapes=[
            pltpu.VMEM((peers, weights.shape[0], weights.shape[1]), jnp.bfloat16),
            pltpu.VMEM((rows, width), jnp.bfloat16),
            pltpu.VMEM((text_rows, width), jnp.bfloat16),
            pltpu.VMEM((chips, rows, wide), jnp.bfloat16),
            pltpu.VMEM((chips, text_rows, wide), jnp.bfloat16),
            pltpu.VMEM((rows, 3 * head_width), jnp.float32),
            pltpu.VMEM((text_rows, 2 * head_width), jnp.float32),
            pltpu.VMEM((peers, 2 * comps, wide), jnp.float32),
            pltpu.VMEM((peers, 2 * comps, wide), jnp.float32),
            pltpu.VMEM((peers, 1, rows), jnp.int32),
            *ring_sems(chips),
            *[dma((chips, 2)) for _ in range(4)],
            *[dma((peers,)) for _ in range(6)],
            dma((5,)),
        ],
        compiler_params=pltpu.CompilerParams(
            collective_id=0, has_side_effects=True, vmem_limit_bytes=VMEM_LIMIT
        ),
        name="project",
    )(weights, image, text, label_row, label, partial_mod)
    out_rows = rows // 8
    half_rows = out_rows // 2
    return tuple(
        pl.pallas_call(
            functools.partial(attend_kernel, peers),
            out_shape=(
                jax.ShapeDtypeStruct(latent.shape, jnp.float32),
                jax.ShapeDtypeStruct(latent.shape, jnp.float32),
            ),
            in_specs=[any_spec, any_spec, any_spec]
            + [vmem] * 6
            + [pl.BlockSpec(memory_space=pltpu.SMEM)],
            out_specs=(vmem, vmem),
            scratch_shapes=[
                pltpu.VMEM((peers, block_rows, 2 * head_width), jnp.bfloat16),
                pltpu.VMEM((8, head_width, width), jnp.bfloat16),
                pltpu.VMEM((head_width // HD, rows, HD), jnp.float32),
                pltpu.VMEM((head_width // HD, rows, HD), jnp.float32),
                pltpu.VMEM((8, out_rows, head_width), jnp.bfloat16),
                pltpu.VMEM((8, out_rows, head_width), jnp.bfloat16),
                pltpu.VMEM((out_rows, width), jnp.float32),
                pltpu.VMEM((out_rows, width), jnp.bfloat16),
                pltpu.VMEM((out_rows, latent.shape[1]), jnp.float32),
                pltpu.VMEM((half_rows, latent.shape[1]), jnp.float32),
                *ring_sems(chips),
                dma((6,)),
                dma((6,)),
                dma((8,)),
                dma((8,)),
                dma((16,)),
                dma((16,)),
                dma((8,)),
                dma((8,)),
                dma,
                dma,
                dma((3,)),
            ],
            compiler_params=pltpu.CompilerParams(
                collective_id=1, has_side_effects=True, vmem_limit_bytes=VMEM_LIMIT
            ),
            name="attend",
        )(
            key_values,
            out_weight,
            image,
            queries,
            label,
            labels,
            mod,
            final_weight,
            latent,
            sig_next - sig_now,
        )
    )


def solution(mesh):
    return jax.shard_map(
        functools.partial(per_device, mesh.shape["req"]),
        mesh=mesh,
        in_specs=(
            P("cfg", "req", None),
            P("cfg", "req", None),
            P(("req", "tp", "cfg"), None),
            P("req"),
            P(),
            P("req", None, None),
            P("req", None, "tp"),
            P("req", None, "tp"),
            P("tp", None),
            P(),
        ),
        out_specs=(P(("req", "tp", "cfg"), None), P(("req", "tp", "cfg"), None)),
        check_vma=False,
    )
```

```python
import functools
import math

import jax
import jax.numpy as jnp
from jax import lax
from jax.experimental import pallas as pl
from jax.experimental.pallas import tpu as pltpu
from jax.sharding import PartitionSpec as P

HD = 128
TEMB = 256
TXT = 512
STEPS = 28
REQS = 4
GUIDE_SCALE = 4.0
MESH = pl.DeviceIdType.MESH
VMEM_LIMIT = 66_000_000
LEAD = 32


def sigma(index):
    linear = 1.0 - index.astype(jnp.float32) / STEPS
    return 3.0 * linear / (1.0 + 2.0 * linear)


def time_features(sigmas):
    half_width = TEMB // 2
    frequency = jnp.exp(-jnp.log(10000.0) * jnp.arange(half_width, dtype=jnp.float32) / half_width)
    angles = 1000.0 * sigmas[:, None] * frequency[None, :]
    features = jnp.concatenate([jnp.cos(angles), jnp.sin(angles)], axis=1)
    return jax.nn.silu(features).astype(jnp.bfloat16)


def rms_heads(value):
    parts = []
    for h in range(value.shape[1] // HD):
        part = value[:, h * HD : (h + 1) * HD]
        mean = jnp.mean(part * part, axis=-1, keepdims=True)
        parts.append((part * lax.rsqrt(mean + 1e-06)).astype(jnp.bfloat16))
    return jnp.concatenate(parts, axis=1)


class Ring:
    def __init__(self, own, held, z, c, chips, sems, lead=0, cfg=0, pair_sems=None):
        self.own, self.held, self.z, self.c, self.chips = own, held, z, c, chips
        self.send, self.recv, self.sib_send, self.sib_recv = sems
        self.half = held.shape[1] // 2
        self.lead, self.cfg, self.pair_sems = lead, cfg, pair_sems

    def rows(self, h):
        if not self.lead:
            return pl.ds(h * self.half, self.half)
        start = pl.multiple_of(h * self.half + self.lead * self.cfg, self.lead)
        return pl.ds(start, self.half - self.lead)

    def pair_rows(self, h, cfg):
        start = pl.multiple_of(h * self.half + (self.half - self.lead) * cfg, self.lead)
        return pl.ds(start, self.lead)

    def pair(self, k, h, cfg):
        slot = self.held.at[2 * self.origin(k) + self.c, self.pair_rows(h, cfg)]
        return pltpu.make_async_remote_copy(
            slot,
            slot,
            self.pair_sems[0].at[k, h],
            self.pair_sems[1].at[k, h],
            device_id={"cfg": 1 - self.cfg},
            device_id_type=MESH,
        )

    def pair_sibling(self, k, h, core):
        slot = self.held.at[2 * self.origin(k) + core, self.pair_rows(h, 1 - self.cfg)]
        return pltpu.make_async_remote_copy(
            slot,
            slot,
            self.pair_sems[2].at[k, h],
            self.pair_sems[3].at[k, h],
            device_id={"req": 2 * self.z + 1 - self.c},
            device_id_type=MESH,
        )

    def chunks(self, s, h):
        return [2 * s - 1, 2 * s] if s < self.chips // 2 else [2 * s - 1]

    def relay(self, s, h):
        for k in self.chunks(s, h):
            self.pair(k, h, 1 - self.cfg).wait_recv()
            self.pair_sibling(k, h, self.c).start()

    def copy(self, d, s, h):
        sign = 1 if d == 0 else -1
        origin = lax.rem(self.z - sign * (s - 1) + self.chips, self.chips)
        target = lax.rem(self.z + sign + self.chips, self.chips)
        slot = self.held.at[2 * origin + self.c, self.rows(h)]
        source = self.own.at[self.rows(h)] if s == 1 else slot
        return pltpu.make_async_remote_copy(
            source,
            slot,
            self.send.at[d, s - 1, h],
            self.recv.at[d, s - 1, h],
            device_id={"req": 2 * target + self.c},
            device_id_type=MESH,
        )

    def arrived(self, d, s, h):
        sign = 1 if d == 0 else -1
        origin = lax.rem(self.z - sign * s + self.chips, self.chips)
        slot = self.held.at[2 * origin + self.c, self.rows(h)]
        return pltpu.make_async_remote_copy(
            slot,
            slot,
            self.send.at[d, s - 1, h],
            self.recv.at[d, s - 1, h],
            device_id={"req": 2 * self.z + 1 - self.c},
            device_id_type=MESH,
        )

    def origin(self, k):
        step = (k + 1) // 2
        sign = 1 if k % 2 == 1 else -1
        return lax.rem(self.z - sign * step + self.chips, self.chips)

    def sibling(self, k, h, core):
        rows = pl.ds(h * self.half, self.half) if k == 0 else self.rows(h)
        slot = self.held.at[2 * self.origin(k) + core, rows]
        source = self.own.at[rows] if k == 0 else slot
        return pltpu.make_async_remote_copy(
            source,
            slot,
            self.sib_send.at[k, h],
            self.sib_recv.at[k, h],
            device_id={"req": 2 * self.z + 1 - self.c},
            device_id_type=MESH,
        )

    def start(self):
        for h in range(2):
            for d in range(2):
                self.copy(d, 1, h).start()
        for h in range(2):
            self.sibling(0, h, self.c).start()

    def poll(self, s, h):
        last = self.chips // 2
        for d in range(2):
            if s == last and h != d:
                continue
            self.arrived(d, s, h).wait_recv()
            if s + 1 < last or (s + 1 == last and h == d):
                self.copy(d, s + 1, h).start()
            k = 2 * s - 1 + (d if s < last else 0)
            if self.lead:
                self.pair(k, h, self.cfg).start()
            self.sibling(k, h, self.c).start()

    def take(self, k):
        for h in range(2):
            self.sibling(k, h, 1 - self.c).wait_recv()
            if self.lead and k:
                self.pair_sibling(k, h, 1 - self.c).wait_recv()

    def finish(self):
        last = self.chips // 2
        for s in range(1, last + 1):
            for h in range(2):
                for d in range(2):
                    if s < last or h == d:
                        self.copy(d, s, h).wait_send()
        for k in range(self.chips):
            for h in range(2):
                self.sibling(k, h, self.c).wait_send()
                if self.lead and k:
                    self.pair(k, h, self.cfg).wait_send()
                    self.pair_sibling(k, h, self.c).wait_send()


def ring_sems(chips):
    return [
        pltpu.SemaphoreType.DMA((2, chips // 2, 2)),
        pltpu.SemaphoreType.DMA((2, chips // 2, 2)),
        pltpu.SemaphoreType.DMA((chips, 2)),
        pltpu.SemaphoreType.DMA((chips, 2)),
    ]


def project_kernel(
    peers,
    w_ref,
    image_ref,
    text_ref,
    label_row_ref,
    label_ref,
    partial_ref,
    q_ref,
    kv_ref,
    labels_ref,
    mod_ref,
    held,
    image,
    text,
    ready,
    text_ready,
    acc,
    text_acc,
    parts,
    mod,
    labels,
    send,
    recv,
    sib_send,
    sib_recv,
    pair_send,
    pair_recv,
    pair_sib_send,
    pair_sib_recv,
    part_send,
    part_recv,
    mod_send,
    mod_recv,
    lab_send,
    lab_recv,
    local,
):
    me = lax.axis_index("req")
    plane = 2 * lax.axis_index("tp") + lax.axis_index("cfg")
    z, c = me // 2, lax.rem(me, 2)
    chips = peers // 2
    rows, width = image.shape
    text_rows = text.shape[0]
    head_width = q_ref.shape[1]
    wide = width // chips

    def in_plane(k):
        target = lax.rem(plane + k, peers)
        return {"tp": target // 2, "cfg": lax.rem(target, 2)}

    barrier = pltpu.get_barrier_semaphore()
    for k in range(1, peers):
        for peer in ({"req": lax.rem(me + k, peers)}, in_plane(k)):
            pl.semaphore_signal(barrier, inc=1, device_id=peer, device_id_type=MESH)
    pl.semaphore_wait(barrier, 2 * (peers - 1))

    ring = Ring(
        w_ref, held, z, c, chips, (send, recv, sib_send, sib_recv), LEAD, lax.axis_index("cfg"),
        (pair_send, pair_recv, pair_sib_send, pair_sib_recv),
    )

    def part_copy(k):
        target = lax.rem(me + k, peers)
        return pltpu.make_async_remote_copy(
            partial_ref.at[plane], parts.at[k], part_send.at[k], part_recv.at[k],
            device_id={"req": target}, device_id_type=MESH,
        )

    def mod_copy(k, owner):
        return pltpu.make_async_remote_copy(
            mod.at[owner], mod.at[owner], mod_send.at[k], mod_recv.at[k],
            device_id=in_plane(k), device_id_type=MESH,
        )

    def label_copy(k, owner):
        return pltpu.make_async_remote_copy(
            label_row_ref, labels.at[owner], lab_send.at[k], lab_recv.at[k],
            device_id={"req": lax.rem(me + k, peers)}, device_id_type=MESH,
        )

    for k in range(1, peers):
        part_copy(k).start()
    ring.start()
    own_part = pltpu.make_async_copy(partial_ref.at[plane], parts.at[0], local.at[0])
    own_part.start()
    image_in = pltpu.make_async_copy(image_ref, image, local.at[1])
    image_in.start()
    text_in = pltpu.make_async_copy(text_ref, text, local.at[2])
    text_in.start()
    own_w = pltpu.make_async_copy(w_ref, held.at[me], local.at[3])
    own_w.start()
    own_label = pltpu.make_async_copy(label_row_ref, labels.at[me], local.at[4])
    own_label.start()
    for k in range(1, peers):
        label_copy(k, me).start()

    own_part.wait()
    for k in range(1, peers):
        part_copy(k).wait_recv()
    total = parts[0]
    for k in range(1, peers):
        total = total + parts[k]
    mod[plane] = total
    for k in range(1, peers):
        mod_copy(k, plane).start()
    image_in.wait()
    text_in.wait()
    for k in range(1, peers):
        mod_copy(k, lax.rem(plane - k + peers, peers)).wait_recv()

    def mod_row(request, component, chunk):
        return mod[2 * chunk + request // 2, 5 * (request % 2) + component : 5 * (request % 2) + component + 1, :]

    tile = 32

    def image_tile(i, carry):
        span = pl.ds(i * tile, tile)
        value = image[span, :].astype(jnp.float32)
        center = value - jnp.mean(value, axis=-1, keepdims=True)
        rstd = lax.rsqrt(jnp.mean(center * center, axis=-1, keepdims=True) + 1e-06)
        label = label_ref[span, :]
        for chunk in range(chips):
            shift = mod_row(REQS - 1, 0, chunk)
            scale = mod_row(REQS - 1, 1, chunk)
            for request in range(REQS - 2, -1, -1):
                mine = label == request
                shift = jnp.where(mine, mod_row(request, 0, chunk), shift)
                scale = jnp.where(mine, mod_row(request, 1, chunk), scale)
            part = center[:, chunk * wide : (chunk + 1) * wide] * rstd
            ready[chunk, span, :] = (part * (1.0 + scale) + shift).astype(jnp.bfloat16)
        return carry

    text_request = me * text_rows // TXT
    text_base = text_request // 2
    text_half = 5 * lax.rem(text_request, 2)

    def text_tile(i, carry):
        span = pl.ds(i * tile, tile)
        value = text[span, :].astype(jnp.float32)
        center = value - jnp.mean(value, axis=-1, keepdims=True)
        rstd = lax.rsqrt(jnp.mean(center * center, axis=-1, keepdims=True) + 1e-06)
        for chunk in range(chips):
            shift = mod[2 * chunk + text_base, pl.ds(text_half + 3, 1), :]
            scale = mod[2 * chunk + text_base, pl.ds(text_half + 4, 1), :]
            part = center[:, chunk * wide : (chunk + 1) * wide] * rstd
            text_ready[chunk, span, :] = (part * (1.0 + scale) + shift).astype(jnp.bfloat16)
        return carry

    image_width = 3 * head_width
    block = w_ref.shape[0]
    mtile = 256

    def multiply(k):
        chip = ring.origin(k)

        def one(i, carry):
            span = pl.ds(i * mtile, mtile)
            lhs = ready[chip, span, :]
            rhs = held[pl.ds(2 * chip, 2), :, :image_width].reshape(2 * block, image_width)
            product = jnp.dot(lhs, rhs, preferred_element_type=jnp.float32)
            acc[span, :] = product if k == 0 else acc[span, :] + product
            return carry

        lax.fori_loop(0, rows // mtile, one, 0)
        text_product = jnp.dot(
            text_ready[chip],
            held[pl.ds(2 * chip, 2), :, image_width:].reshape(2 * block, 2 * head_width),
            preferred_element_type=jnp.float32,
        )
        text_acc[...] = text_product if k == 0 else text_acc[...] + text_product

    lax.fori_loop(0, text_rows // tile, text_tile, 0)
    ring.poll(1, 0)
    lax.fori_loop(0, rows // tile // 2, image_tile, 0)
    ring.poll(1, 1)
    lax.fori_loop(rows // tile // 2, rows // tile, image_tile, 0)
    own_w.wait()
    ring.take(0)
    multiply(0)
    last = chips // 2
    for s in range(2, last + 1):
        ring.poll(s, 0)
        if s == 2:
            ring.relay(1, 0)
        ring.relay(s - 1, 1)
        ring.take(2 * s - 3)
        multiply(2 * s - 3)
        ring.poll(s, 1)
        ring.relay(s, 0)
        ring.take(2 * s - 2)
        multiply(2 * s - 2)
    ring.relay(last, 1)
    ring.take(chips - 1)
    multiply(chips - 1)

    def finish_tile(i, carry):
        span = pl.ds(i * mtile, mtile)
        q_ref[span, :] = rms_heads(acc[span, :head_width])
        kv_ref[span, :head_width] = rms_heads(acc[span, head_width : 2 * head_width])
        kv_ref[span, head_width:] = acc[span, 2 * head_width :].astype(jnp.bfloat16)
        return carry

    lax.fori_loop(0, rows // mtile, finish_tile, 0)
    kv_ref[rows:, :head_width] = rms_heads(text_acc[:, :head_width])
    kv_ref[rows:, head_width:] = text_acc[:, head_width:].astype(jnp.bfloat16)
    own_label.wait()
    for k in range(1, peers):
        label_copy(k, lax.rem(me - k + peers, peers)).wait_recv()
    labels_ref[...] = labels[...]
    mod_ref[...] = mod[...]
    for k in range(1, peers):
        part_copy(k).wait_send()
        mod_copy(k, plane).wait_send()
        label_copy(k, me).wait_send()
    ring.finish()


def attend_kernel(
    peers,
    kv_ref,
    out_w_ref,
    image_ref,
    q_ref,
    label_ref,
    labels_ref,
    mod_ref,
    final_ref,
    latent_ref,
    dsig_ref,
    guided_ref,
    next_ref,
    held,
    out_w,
    numer,
    denom,
    attended,
    gathered,
    update,
    image,
    velocity,
    other_velocity,
    send,
    recv,
    sib_send,
    sib_recv,
    x_send,
    x_recv,
    y_send,
    y_recv,
    ws_send,
    ws_recv,
    a_send,
    a_recv,
    v_send,
    v_recv,
    local,
):
    me = lax.axis_index("req")
    tp = lax.axis_index("tp")
    cfg = lax.axis_index("cfg")
    z, c = me // 2, lax.rem(me, 2)
    chips = peers // 2
    y, x = tp // 4, lax.rem(tp, 4)
    rows, head_width = q_ref.shape
    heads = head_width // HD
    block = held.shape[1]
    right = lax.rem(x + 1, 4)
    left = lax.rem(x + 3, 4)
    flip = lax.rem(tp + 4, 8)

    barrier = pltpu.get_barrier_semaphore()
    greet = [
        {"req": 2 * lax.rem(z + 1, chips) + c},
        {"req": 2 * lax.rem(z + chips - 1, chips) + c},
        {"req": 2 * z + 1 - c},
        {"cfg": 1 - cfg, "tp": flip},
        {"cfg": 1 - cfg},
    ] + [{"tp": lax.rem(tp + k, 8)} for k in range(1, 8)]
    for peer in greet:
        pl.semaphore_signal(barrier, inc=1, device_id=peer, device_id_type=MESH)
    pl.semaphore_wait(barrier, len(greet))

    ring = Ring(kv_ref, held, z, c, chips, (send, recv, sib_send, sib_recv))
    ring.start()
    own_kv = pltpu.make_async_copy(kv_ref, held.at[me], local.at[0])
    own_kv.start()

    piece = out_w.shape[1] // 4

    def w_rows(core, h):
        return pl.ds(core * 2 * piece + h * piece, piece)

    def w_copy(source, shard, core, h, sems, index, peer):
        slot = out_w.at[shard, w_rows(core, h)]
        return pltpu.make_async_remote_copy(
            slot if source is None else source,
            slot,
            sems[0].at[index],
            sems[1].at[index],
            device_id=peer,
            device_id_type=MESH,
        )

    xs, ys, ws = (x_send, x_recv), (y_send, y_recv), (ws_send, ws_recv)
    across = [x, left, right, lax.rem(x + 2, 4)]
    to_right, to_left = {"tp": y * 4 + right}, {"tp": y * 4 + left}
    to_y = [{"tp": flip}, {"cfg": 1 - cfg, "tp": flip}]
    to_sibling = {"req": 2 * z + 1 - c}
    own_piece = [out_w_ref.at[w_rows(c, h)] for h in range(2)]

    def x_copy(d, h):
        return w_copy(own_piece[h], tp, c, h, xs, 2 * d + h, to_right if d == 0 else to_left)

    def x_arrived(d, h):
        return w_copy(None, y * 4 + (left if d == 0 else right), c, h, xs, 2 * d + h, to_sibling)

    def x_forward(d):
        return w_copy(None, y * 4 + (left if d == 0 else right), c, d, xs, 4 + d, to_right if d == 0 else to_left)

    def x_forwarded(d):
        return w_copy(None, y * 4 + across[3], c, d, xs, 4 + d, to_sibling)

    def y_copy(n, h):
        return w_copy(own_piece[h] if n == 0 else None, y * 4 + across[n], c, h, ys, 2 * n + h, to_y[h])

    def y_arrived(n, h):
        return w_copy(None, (1 - y) * 4 + across[n], c, h, ys, 2 * n + h, to_sibling)

    def w_sibling(n, h, core):
        shard = y * 4 + across[n] if n < 4 else (1 - y) * 4 + across[n - 4]
        return w_copy(None, shard, core, h, ws, 2 * n + h, to_sibling)

    for h in range(2):
        for d in range(2):
            x_copy(d, h).start()
        y_copy(0, h).start()
    own_out = pltpu.make_async_copy(out_w_ref, out_w.at[tp], local.at[1])
    own_out.start()
    out_rows = rows // 8
    own_image = pltpu.make_async_copy(
        image_ref.at[pl.ds(tp * out_rows, out_rows)], image, local.at[2]
    )
    own_image.start()
    numer[...] = jnp.zeros_like(numer)
    denom[...] = jnp.zeros_like(denom)

    def x_events():
        for h in range(2):
            for d in range(2):
                x_arrived(d, h).wait_recv()
                if h == d:
                    x_forward(d).start()
                y_copy(1 + d, h).start()
                w_sibling(1 + d, h, c).start()

    def x_more():
        for d in range(2):
            x_forwarded(d).wait_recv()
            y_copy(3, d).start()
            w_sibling(3, d, c).start()

    def y_events(n):
        for h in range(2):
            y_arrived(n, h).wait_recv()
            w_sibling(4 + n, h, c).start()

    factor = HD ** (-0.5) * math.log2(math.e)
    qtile = 256
    text_keys = block - rows

    def attend(k):
        chip = ring.origin(k)

        def one(i, carry):
            b = 2 * chip + i // (rows // qtile)
            span = pl.ds(lax.rem(i, rows // qtile) * qtile, qtile)
            text_label = jnp.full((1, text_keys), b * text_keys // TXT, jnp.int32)
            key_label = jnp.concatenate([labels_ref[b], text_label], axis=1)
            allowed = label_ref[span, :] == key_label
            for h in range(heads):
                q = q_ref[span, h * HD : (h + 1) * HD]
                key = held[b, :, h * HD : (h + 1) * HD]
                value = held[b, :, head_width + h * HD : head_width + (h + 1) * HD]
                scores = lax.dot_general(
                    q, key, (((1,), (1,)), ((), ())), preferred_element_type=jnp.float32
                )
                weights = jnp.where(allowed, jnp.exp2(scores * factor), 0.0)
                part = weights[:, :HD]
                for j in range(1, block // HD):
                    part = part + weights[:, j * HD : (j + 1) * HD]
                denom[h, span, :] += part
                numer[h, span, :] += jnp.dot(
                    weights.astype(jnp.bfloat16), value, preferred_element_type=jnp.float32
                )
            return carry

        lax.fori_loop(0, 2 * (rows // qtile), one, 0)

    own_kv.wait()
    ring.take(0)
    attend(0)
    ring.poll(1, 0)
    ring.poll(1, 1)
    last = chips // 2
    for s in range(2, last):
        ring.poll(s, 0)
        if s == 2:
            x_events()
        ring.take(2 * s - 3)
        attend(2 * s - 3)
        if s == 3:
            x_more()
            y_events(0)
        ring.poll(s, 1)
        ring.take(2 * s - 2)
        attend(2 * s - 2)
        if s == 3:
            y_events(1)
            y_events(2)
    ring.take(chips - 3)
    attend(chips - 3)
    ring.poll(last, 0)
    ring.take(chips - 2)
    attend(chips - 2)
    ring.poll(last, 1)
    y_events(3)
    ring.take(chips - 1)
    attend(chips - 1)

    for h in range(heads):
        total = jnp.sum(denom[h], axis=-1, keepdims=True)
        value = (numer[h] / total).astype(jnp.bfloat16)
        for t in range(8):
            attended[t, :, h * HD : (h + 1) * HD] = value[t * out_rows : (t + 1) * out_rows]

    def a_copy(k, owner):
        target = lax.rem(tp + k, 8)
        return pltpu.make_async_remote_copy(
            attended.at[target], gathered.at[owner], a_send.at[k], a_recv.at[k],
            device_id={"tp": target}, device_id_type=MESH,
        )

    for k in range(1, 8):
        a_copy(k, tp).start()
    gathered[tp] = attended[tp]

    own_out.wait()
    own_image.wait()
    for n in range(1, 8):
        for h in range(2):
            w_sibling(n, h, 1 - c).wait_recv()
    update[...] = jnp.dot(gathered[tp], out_w[tp], preferred_element_type=jnp.float32)
    for k in range(1, 8):
        a_copy(k, lax.rem(tp - k + 8, 8)).wait_recv()

    def add_shard(k, carry):
        t = lax.rem(tp + k, 8)
        update[...] += jnp.dot(gathered[t], out_w[t], preferred_element_type=jnp.float32)
        return carry

    lax.fori_loop(1, 8, add_shard, 0)

    width = update.shape[1]
    wide = width // chips
    label = label_ref[pl.ds(pl.multiple_of(tp * out_rows, out_rows), out_rows), :]
    masks = [label == request for request in range(REQS - 1)]
    mean = jnp.zeros((out_rows, 1), jnp.float32)
    for chunk in range(chips):
        cols = slice(chunk * wide, (chunk + 1) * wide)

        def gate_row(request):
            row = 5 * (request % 2) + 2
            return mod_ref[2 * chunk + request // 2, row : row + 1, :]

        gate = gate_row(REQS - 1)
        for request in range(REQS - 2, -1, -1):
            gate = jnp.where(masks[request], gate_row(request), gate)
        stream = image[:, cols].astype(jnp.float32) + gate * update[:, cols]
        update[:, cols] = stream
        mean = mean + jnp.sum(stream, axis=-1, keepdims=True)
    center = update[...] - mean / width
    normed = center * lax.rsqrt(jnp.mean(center * center, axis=-1, keepdims=True) + 1e-06)
    velocity[...] = lax.dot_general(
        normed.astype(jnp.bfloat16), final_ref[...], (((1,), (1,)), ((), ())),
        preferred_element_type=jnp.float32,
    )
    half_rows = out_rows // 2
    sent = pl.ds(pl.multiple_of((1 - cfg) * half_rows, half_rows), half_rows)
    kept = pl.ds(pl.multiple_of(cfg * half_rows, half_rows), half_rows)
    swap = pltpu.make_async_remote_copy(
        velocity.at[sent], other_velocity, v_send, v_recv,
        device_id={"cfg": 1 - cfg}, device_id_type=MESH,
    )
    swap.start()
    own = velocity[kept, :]
    own_label = label_ref[pl.ds(pl.multiple_of(tp * out_rows + cfg * half_rows, half_rows), half_rows), :]
    step = jnp.where(
        own_label == 0,
        dsig_ref[0],
        jnp.where(own_label == 1, dsig_ref[1], jnp.where(own_label == 2, dsig_ref[2], dsig_ref[3])),
    )
    swap.wait()
    other = other_velocity[...]
    first = cfg == 0
    cond = jnp.where(first, own, other)
    uncond = jnp.where(first, other, own)
    guided = uncond + GUIDE_SCALE * (cond - uncond)
    guided_ref[...] = guided
    next_ref[...] = latent_ref[...] + step * guided

    for h in range(2):
        for d in range(2):
            x_copy(d, h).wait_send()
    for d in range(2):
        x_forward(d).wait_send()
    for n in range(4):
        for h in range(2):
            y_copy(n, h).wait_send()
    for n in range(1, 8):
        for h in range(2):
            w_sibling(n, h, c).wait_send()
    for k in range(1, 8):
        a_copy(k, tp).wait_send()
    ring.finish()


def per_device(
    peers,
    img_hidden,
    txt_hidden,
    latent,
    segment,
    timestep,
    mod_weight,
    qkv_weight,
    txt_kv_weight,
    out_weight,
    final_weight,
):
    image = img_hidden[0]
    text = txt_hidden[0]
    rows, width = image.shape
    text_rows = text.shape[0]
    shard, comps = mod_weight.shape[:2]
    chips = peers // 2
    wide = width // chips
    head_width = qkv_weight.shape[2]
    block_rows = rows + text_rows
    sig_now = sigma(timestep)
    sig_next = sigma(timestep + 1)
    features = time_features(sig_now)
    feature_part = lax.dynamic_slice_in_dim(features, lax.axis_index("req") * shard, shard, 1)
    partial_mod = jnp.einsum(
        "rj,jkd->rkd", feature_part, mod_weight, preferred_element_type=jnp.float32
    )
    partial_mod = (
        partial_mod.reshape(2, 2 * comps, chips, wide).transpose(2, 0, 1, 3)
    ).reshape(peers, 2 * comps, wide)
    weights = jnp.concatenate(
        [
            qkv_weight.reshape(qkv_weight.shape[0], 3 * head_width),
            txt_kv_weight.reshape(qkv_weight.shape[0], 2 * head_width),
        ],
        axis=1,
    )
    label_row = segment.reshape(1, rows)
    label = segment.reshape(rows, 1)
    any_spec = pl.BlockSpec(memory_space=pl.ANY)
    vmem = pl.BlockSpec(memory_space=pltpu.VMEM)
    dma = pltpu.SemaphoreType.DMA
    queries, key_values, labels, mod = pl.pallas_call(
        functools.partial(project_kernel, peers),
        out_shape=(
            jax.ShapeDtypeStruct((rows, head_width), jnp.bfloat16),
            jax.ShapeDtypeStruct((block_rows, 2 * head_width), jnp.bfloat16),
            jax.ShapeDtypeStruct((peers, 1, rows), jnp.int32),
            jax.ShapeDtypeStruct((peers, 2 * comps, wide), jnp.float32),
        ),
        in_specs=[any_spec, any_spec, any_spec, vmem, vmem, vmem],
        out_specs=(vmem, vmem, vmem, vmem),
        scratch_shapes=[
            pltpu.VMEM((peers, weights.shape[0], weights.shape[1]), jnp.bfloat16),
            pltpu.VMEM((rows, width), jnp.bfloat16),
            pltpu.VMEM((text_rows, width), jnp.bfloat16),
            pltpu.VMEM((chips, rows, wide), jnp.bfloat16),
            pltpu.VMEM((chips, text_rows, wide), jnp.bfloat16),
            pltpu.VMEM((rows, 3 * head_width), jnp.float32),
            pltpu.VMEM((text_rows, 2 * head_width), jnp.float32),
            pltpu.VMEM((peers, 2 * comps, wide), jnp.float32),
            pltpu.VMEM((peers, 2 * comps, wide), jnp.float32),
            pltpu.VMEM((peers, 1, rows), jnp.int32),
            *ring_sems(chips),
            *[dma((chips, 2)) for _ in range(4)],
            *[dma((peers,)) for _ in range(6)],
            dma((5,)),
        ],
        compiler_params=pltpu.CompilerParams(
            collective_id=0, has_side_effects=True, vmem_limit_bytes=VMEM_LIMIT
        ),
        name="project",
    )(weights, image, text, label_row, label, partial_mod)
    out_rows = rows // 8
    half_rows = out_rows // 2
    return tuple(
        pl.pallas_call(
            functools.partial(attend_kernel, peers),
            out_shape=(
                jax.ShapeDtypeStruct(latent.shape, jnp.float32),
                jax.ShapeDtypeStruct(latent.shape, jnp.float32),
            ),
            in_specs=[any_spec, any_spec, any_spec]
            + [vmem] * 6
            + [pl.BlockSpec(memory_space=pltpu.SMEM)],
            out_specs=(vmem, vmem),
            scratch_shapes=[
                pltpu.VMEM((peers, block_rows, 2 * head_width), jnp.bfloat16),
                pltpu.VMEM((8, head_width, width), jnp.bfloat16),
                pltpu.VMEM((head_width // HD, rows, HD), jnp.float32),
                pltpu.VMEM((head_width // HD, rows, HD), jnp.float32),
                pltpu.VMEM((8, out_rows, head_width), jnp.bfloat16),
                pltpu.VMEM((8, out_rows, head_width), jnp.bfloat16),
                pltpu.VMEM((out_rows, width), jnp.float32),
                pltpu.VMEM((out_rows, width), jnp.bfloat16),
                pltpu.VMEM((out_rows, latent.shape[1]), jnp.float32),
                pltpu.VMEM((half_rows, latent.shape[1]), jnp.float32),
                *ring_sems(chips),
                dma((6,)),
                dma((6,)),
                dma((8,)),
                dma((8,)),
                dma((16,)),
                dma((16,)),
                dma((8,)),
                dma((8,)),
                dma,
                dma,
                dma((3,)),
            ],
            compiler_params=pltpu.CompilerParams(
                collective_id=1, has_side_effects=True, vmem_limit_bytes=VMEM_LIMIT
            ),
            name="attend",
        )(
            key_values,
            out_weight,
            image,
            queries,
            label,
            labels,
            mod,
            final_weight.T,
            latent,
            sig_next - sig_now,
        )
    )


def solution(mesh):
    return jax.shard_map(
        functools.partial(per_device, mesh.shape["req"]),
        mesh=mesh,
        in_specs=(
            P("cfg", "req", None),
            P("cfg", "req", None),
            P(("req", "tp", "cfg"), None),
            P("req"),
            P(),
            P("req", None, None),
            P("req", None, "tp"),
            P("req", None, "tp"),
            P("tp", None),
            P(),
        ),
        out_specs=(P(("req", "tp", "cfg"), None), P(("req", "tp", "cfg"), None)),
        check_vma=False,
    )
```
